32 devices in a mesh: gx: 4 (over x, core), gy: 8 (over z, y).
Axes of the slice: x: 2, y: 2, z: 4, core: 2. Of those that a mesh axis runs over, the one named last changes fastest.
Arguments:
- fields: float32 [9, 32, 128, 128], P(None, 'gx', 'gy'), may hold values from -6 to 6
- labels: int32 [32, 128, 128], P('gx', 'gy'), may hold values from 0 to 7
- buoyancy: float32 [8], replicated, may hold values from 0.15 to 0.35
- lame_first: float32 [8], replicated, may hold values from 0.15 to 0.45
- shear_modulus: float32 [8], replicated, may hold values from 0.05 to 0.2
- relax_rate: float32 [8], replicated, may hold values from 0.02 to 0.3
Outputs:
- advanced: float32 [9, 32, 128, 128], P(None, 'gx', 'gy')
The draws below stay inside these ranges and needn't reach their ends.
Inputs may be any that keep to these rules, and one draw needn't show every extreme that they name: labels name tissue classes.
All inputs are finite; a program needn't handle non-finite values.
Results may differ from the reference program's by a relative error of at most 0.00002.
Values sent between devices are 32-bit elements; how exact they have to be, the bound alone decides.
A program may use at most 64 MiB of HBM per device.

```python
import math
import jax
import jax.numpy as jnp
from jax import lax

NZ = 128
STEPS = 4
LABELS = 8
NX = 32
NY = 128


def touch_ends(drawn, own_key, least, largest):
    shape = drawn.shape
    index_at = [jax.random.randint(jax.random.fold_in(own_key, axis), (), 0, shape[axis]) for axis in range(len(shape))]
    drawn = drawn.at[tuple(index_at)].set(least)
    longest = shape.index(max(shape))
    index_at[longest] = (index_at[longest] + 1) % shape[longest]
    return drawn.at[tuple(index_at)].set(largest)


def shard_levels(stream_key, extent, pieces, low, high):
    loudness, own = 1.0, jax.random.fold_in(stream_key, 6)
    for position, blocks in pieces:
        draws = jnp.exp(jax.random.uniform(jax.random.fold_in(own, position), (blocks,), jnp.float32, low / len(pieces), high / len(pieces)))
        loudness = loudness * jnp.repeat(draws, extent[position] // blocks).reshape([-1 if axis == position else 1 for axis in range(len(extent))])
    return loudness


def centred(own_key, extent, deviation, most, shards=(), kind=jnp.bfloat16):
    values = deviation * jax.random.normal(own_key, extent, jnp.float32)
    if shards:
        values = values * shard_levels(own_key, extent, shards, -0.22, 0.18)
    return jnp.clip(values, -most, most).astype(kind)


def setup_inputs(seed: int = 0) -> dict:
    seeds = jax.random.split(jax.random.key(seed), 7)
    fields = centred(seeds[0], (9, NX, NY, NZ), 1.0, 6.0, ((1, 4), (2, 8)), jnp.float32)
    labels = touch_ends(jax.random.randint(seeds[1], (NX, NY, NZ), 0, LABELS), jax.random.fold_in(seeds[1], 1), 0, LABELS - 1).astype(jnp.int32)
    buoyancy = jnp.clip(jnp.exp(jax.random.uniform(seeds[2], (LABELS,), jnp.float32, math.log(0.15), math.log(0.35))), 0.15, 0.35)
    lame_first = jnp.clip(jnp.exp(jax.random.uniform(seeds[3], (LABELS,), jnp.float32, math.log(0.15), math.log(0.45))), 0.15, 0.45)
    shear_modulus = jnp.clip(jnp.exp(jax.random.uniform(seeds[4], (LABELS,), jnp.float32, math.log(0.05), math.log(0.2))), 0.05, 0.2)
    relax_rate = jnp.clip(jnp.exp(jax.random.uniform(seeds[5], (LABELS,), jnp.float32, math.log(0.02), math.log(0.3))), 0.02, 0.3)
    return dict(fields=fields, labels=labels, buoyancy=buoyancy, lame_first=lame_first, shear_modulus=shear_modulus, relax_rate=relax_rate)


def ahead(field, axis):
    count = field.shape[axis]
    zeros = jnp.zeros_like(lax.slice_in_dim(field, 0, 1, axis=axis))
    following = jnp.concatenate([lax.slice_in_dim(field, 1, count, axis=axis), zeros], axis)
    return following - field


def behind(field, axis):
    count = field.shape[axis]
    zeros = jnp.zeros_like(lax.slice_in_dim(field, 0, 1, axis=axis))
    previous = jnp.concatenate([zeros, lax.slice_in_dim(field, 0, count - 1, axis=axis)], axis)
    return field - previous


def advance(state, moduli, inside):
    speed_x, speed_y, speed_z, stress_xx, stress_yy, stress_zz, stress_xy, stress_xz, stress_yz = state
    buoy, lame, shear, relax = moduli
    speed_x = (speed_x + buoy * (ahead(stress_xx, 0) + behind(stress_xy, 1) + behind(stress_xz, 2))) * inside
    speed_y = (speed_y + buoy * (behind(stress_xy, 0) + ahead(stress_yy, 1) + behind(stress_yz, 2))) * inside
    speed_z = (speed_z + buoy * (behind(stress_xz, 0) + behind(stress_yz, 1) + ahead(stress_zz, 2))) * inside
    strain_xx = behind(speed_x, 0)
    strain_yy = behind(speed_y, 1)
    strain_zz = behind(speed_z, 2)
    spread = strain_xx + strain_yy + strain_zz
    keep = 1.0 - relax
    stress_xx = (keep * stress_xx + lame * spread + 2.0 * shear * strain_xx) * inside
    stress_yy = (keep * stress_yy + lame * spread + 2.0 * shear * strain_yy) * inside
    stress_zz = (keep * stress_zz + lame * spread + 2.0 * shear * strain_zz) * inside
    stress_xy = (keep * stress_xy + shear * (ahead(speed_x, 1) + ahead(speed_y, 0))) * inside
    stress_xz = (keep * stress_xz + shear * (ahead(speed_x, 2) + ahead(speed_z, 0))) * inside
    stress_yz = (keep * stress_yz + shear * (ahead(speed_y, 2) + ahead(speed_z, 1))) * inside
    return [speed_x, speed_y, speed_z, stress_xx, stress_yy, stress_zz, stress_xy, stress_xz, stress_yz]


def reference(fields, labels, buoyancy, lame_first, shear_modulus, relax_rate):
    moduli = [buoyancy[labels], lame_first[labels], shear_modulus[labels], relax_rate[labels]]
    state = [fields[channel] for channel in range(9)]
    for repeat in range(STEPS):
        state = advance(state, moduli, jnp.float32(1.0))
    return jnp.stack(state)
```

```python
import functools

import jax
import jax.numpy as jnp
from jax import lax
from jax.experimental import pallas as pl
from jax.experimental.pallas import tpu as pltpu
from jax.sharding import PartitionSpec as P

STEPS = 4
LABELS = 8
HALO = STEPS
BASE = 8
MESH = pl.DeviceIdType.MESH
VX, VY, VZ, SXX, SYY, SZZ, SXY, SXZ, SYZ = range(9)
GOT = (0, 2, 1, 6, 3, 7, 4, 8, 5)


def kernel(nx, ny, fields, labels, buoy_h, lame_h, shear_h, relax_h, out, got, state, tissue,
           buoy, lame, shear, keep, count, buoy_t, lame_t, shear_t, relax_t, send_sem, recv_sem, local_sem):
    local_x, local_y = labels.shape[0], labels.shape[1]
    gx, gy = lax.axis_index("gx"), lax.axis_index("gy")
    has = {("gx", -1): gx > 0, ("gx", 1): gx < nx - 1, ("gy", -1): gy > 0, ("gy", 1): gy < ny - 1}
    place = {"gx": gx, "gy": gy}
    x0, x1, x2, x3 = 0, HALO, HALO + local_x, local_x + 2 * HALO
    y0, y1, y2, y3 = BASE, BASE + HALO, BASE + HALO + local_y, BASE + local_y + 2 * HALO
    rows = slice(y0, y3)

    barrier = pltpu.get_barrier_semaphore()
    for (axis, way), there in has.items():
        @pl.when(there)
        def _(axis=axis, way=way):
            pl.semaphore_signal(barrier, inc=1, device_id={axis: place[axis] + way}, device_id_type=MESH)

    label_copy = pltpu.make_async_copy(labels, tissue.at[x1:x2, y1:y2], local_sem.at[0])
    label_copy.start()
    tables_copies = [
        pltpu.make_async_copy(source, table, local_sem.at[3 + index])
        for index, (source, table) in enumerate((
            (buoy_h, buoy_t), (lame_h, lame_t), (shear_h, shear_t), (relax_h, relax_t)))]
    for copy in tables_copies:
        copy.start()
    own = pltpu.make_async_copy(fields, state.at[:, x1:x2, y1:y2], local_sem.at[1])
    own.start()
    for f in range(SXX, SYZ + 1):
        pltpu.make_async_copy(fields.at[f], got.at[GOT[f], x1:x2, y1:y2], local_sem.at[2]).start()

    def wait_rows(amount, sem):
        pltpu.make_async_copy(count.at[:amount], count.at[:amount], sem).wait()

    lanes = state.shape[3]

    def blank(a, b, c, d):
        got[:, a:b, c:d] = jnp.zeros((9, b - a, d - c, lanes), jnp.float32)
        tissue[a:b, c:d] = jnp.full((b - a, d - c, lanes), LABELS, jnp.int32)

    pl.when(jnp.logical_not(has["gx", -1]))(lambda: blank(x0, x1, y0, y3))
    pl.when(jnp.logical_not(has["gx", 1]))(lambda: blank(x2, x3, y0, y3))
    pl.when(jnp.logical_not(has["gy", -1]))(lambda: blank(x0, x3, y0, y1))
    pl.when(jnp.logical_not(has["gy", 1]))(lambda: blank(x0, x3, y2, y3))
    for f in (SXY, SYZ):
        state[f, x1:x2, y1 - 1:y1] = jnp.zeros((local_x, 1, lanes), jnp.float32)
    state[SYY, x1:x2, y2:y2 + 1] = jnp.zeros((local_x, 1, lanes), jnp.float32)

    lane = lax.broadcasted_iota(jnp.int32, (y3 - y0, lanes), 1)
    first_z, last_z = lane == 0, lane == lanes - 1

    def ahead_z(a):
        following = pltpu.roll(a, lanes - 1, 1)
        return jnp.where(last_z[:a.shape[0]], 0.0, following) - a

    def behind_z(a):
        return a - jnp.where(first_z[:a.shape[0]], 0.0, pltpu.roll(a, 1, 1))

    def store(stores):
        for ref, index, value in stores:
            ref[index] = value

    label_copy.wait()
    for copy in tables_copies:
        copy.wait()

    @pl.loop(0, local_x)
    def _(p):
        label = tissue[x1 + p, y1:y2]
        table = jnp.zeros(label.shape, jnp.float32)
        for kind in range(LABELS):
            table = jnp.where(label == kind, buoy_t[kind], table)
        buoy[x1 + p, y1 - y0:y2 - y0] = table

    own.wait()

    def alone(p):
        get = lambda f, q=p, shift=0: state[f, q, y1 + shift:y2 + shift]
        b = buoy[p, y1 - y0:y2 - y0]
        sxy, sxz, syz = get(SXY), get(SXZ), get(SYZ)
        xx = get(SXX, p + 1) - get(SXX) if p < x2 - 1 else -get(SXX)
        xy = sxy - get(SXY, p - 1) if p > x1 else sxy
        xz = sxz - get(SXZ, p - 1) if p > x1 else sxz
        vx = get(VX) + b * (xx + (sxy - get(SXY, p, -1)) + behind_z(sxz))
        vy = get(VY) + b * (xy + (get(SYY, p, 1) - get(SYY)) + behind_z(syz))
        vz = get(VZ) + b * (xz + (syz - get(SYZ, p, -1)) + ahead_z(get(SZZ)))
        return [(got, (GOT[f], p, slice(y1, y2)), v) for f, v in ((VX, vx), (VY, vy), (VZ, vz))]

    for p in range(x1, x2, 2):
        store(alone(p) + alone(p + 1))

    wait_rows(6 * local_x * local_y, local_sem.at[2])
    pl.semaphore_wait(barrier, sum(there.astype(jnp.int32) for there in has.values()))

    odd = lax.rem(gx, 2) == 1
    ways = (jnp.where(odd, 1, -1), jnp.where(odd, -1, 1))
    has_x = (jnp.where(odd, gx < nx - 1, gx > 0), jnp.where(odd, gx > 0, gx < nx - 1))

    class Group:
        def __init__(self, send, recv):
            self.send, self.recv, self.copies, self.amount = send_sem.at[send], recv_sem.at[recv], [], 0

        def add(self, source, target, axis, way):
            size = 1
            for extent in source.shape[:-1]:
                size *= extent
            self.amount += size
            self.copies.append(pltpu.make_async_remote_copy(
                src_ref=source, dst_ref=target, send_sem=self.send, recv_sem=self.recv,
                device_id={axis: place[axis] + way}, device_id_type=MESH))
            return self

        def start(self, there):
            @pl.when(there)
            def _():
                for copy in self.copies:
                    copy.start()

        def arrive(self, there):
            pl.when(there)(lambda: wait_rows(self.amount, self.recv))

    def out_rows(way, near, far):
        return slice(y2 - far, y2 - near) if way == 1 else slice(y1 + near, y1 + far)

    def in_rows(way, near, far):
        return slice(y1 - far, y1 - near) if way == 1 else slice(y2 + near, y2 + far)

    def out_planes(way, near, far):
        return pl.ds(jnp.where(way == 1, x2 - far, x1 + near), far - near)

    def in_planes(way, near, far):
        return pl.ds(jnp.where(way == 1, x1 - far, x2 + near), far - near)

    def over_y(group, way, fs, planes, near, far):
        a, b = out_rows(way, near, far), in_rows(way, near, far)
        group.add(got.at[fs, planes, a], got.at[fs, planes, b], "gy", way)

    sides = (-1, 1)
    everything = slice(0, 9)
    labels_y, labels_x, early, late, faces, corner_labels, corners = {}, {}, {}, {}, {}, {}, {}
    for s, way in enumerate(sides):
        labels_y[way] = Group(s, s).add(
            tissue.at[x1:x2, out_rows(way, 0, HALO)], tissue.at[x1:x2, in_rows(way, 0, HALO)], "gy", way)
        a, b = (x2 - HALO, x1 - HALO) if way == 1 else (x1, x2)
        labels_x[way] = Group(2 + s, 2 + s).add(
            tissue.at[a:a + HALO, y1:y2], tissue.at[b:b + HALO, y1:y2], "gx", way)
        late[way] = Group(s, 4 + s)
        over_y(late[way], way, slice(0, 6) if way == 1 else everything, slice(x1 + 1, x2 - 1), 2, 3)
        over_y(late[way], way, slice(2, 3) if way == 1 else slice(0, 2), slice(x1, x2), 3, 4)
        faces[way] = Group(2 + s, 6 + s)
        for fs, near, far in ((everything, 0, 3), (slice(0, 1) if way == 1 else slice(1, 3), 3, 4)):
            a, b = (x2 - far, x1 - far) if way == 1 else (x1 + near, x2 + near)
            faces[way].add(got.at[fs, a:a + far - near, y1:y2], got.at[fs, b:b + far - near, y1:y2], "gx", way)
        for k, x_way in enumerate(ways):
            lone = pl.ds(GOT[SXY] if way == 1 else jnp.where(x_way == 1, GOT[SXZ], GOT[SXX]), 1)
            parts = ((everything, 0, 1, 0, 3), (everything, 1, 4, 0, 2), (lone, 0, 1, 3, 4))
            early[k, way] = Group(s, 8 + 2 * k + s)
            corner_labels[k, way] = Group(4 + 2 * k + s, 12 + 2 * k + s).add(
                tissue.at[out_planes(x_way, 0, 3), in_rows(way, 0, 3)],
                tissue.at[in_planes(x_way, 0, 3), in_rows(way, 0, 3)], "gx", x_way)
            corners[k, way] = Group(4 + 2 * k + s, 16 + 2 * k + s)
            for fs, x_near, x_far, near, far in parts:
                over_y(early[k, way], way, fs, out_planes(x_way, x_near, x_far), near, far)
                corners[k, way].add(
                    got.at[fs, out_planes(x_way, x_near, x_far), in_rows(way, near, far)],
                    got.at[fs, in_planes(x_way, x_near, x_far), in_rows(way, near, far)], "gx", x_way)

    for way in sides:
        labels_y[way].start(has["gy", way])
    for k in range(2):
        for way in sides:
            early[k, way].start(has["gy", way])
    for way in sides:
        labels_x[way].start(has["gx", way])
    for way in sides:
        faces[way].start(has["gx", way])
    for way in sides:
        late[way].start(has["gy", way])

    for way in sides:
        labels_y[way].arrive(has["gy", -way])
        for k in range(2):
            corner_labels[k, way].start(has["gy", -way] & has_x[k])
    for way in sides:
        labels_x[way].arrive(has["gx", -way])
        for k in range(2):
            corner_labels[k, way].arrive(has["gy", -way] & has_x[k])

    @pl.loop(0, x3 - x0)
    def _(p):
        label = tissue[p, rows]
        tables = [jnp.zeros(label.shape, jnp.float32) for _ in range(4)]
        for kind in range(LABELS):
            here = label == kind
            values = (buoy_t[kind], lame_t[kind], shear_t[kind], 1.0 - relax_t[kind])
            tables = [jnp.where(here, value, old) for value, old in zip(values, tables)]
        for ref, table in zip((buoy, lame, shear, keep), tables):
            ref[p] = table

    for k in range(2):
        for way in sides:
            early[k, way].arrive(has["gy", -way])
            corners[k, way].start(has["gy", -way] & has_x[k])
    for way in sides:
        faces[way].arrive(has["gx", -way])
    for way in sides:
        late[way].arrive(has["gy", -way])
    for k in range(2):
        for way in sides:
            corners[k, way].arrive(has["gy", -way] & has_x[k])

    tall = y3 - y0
    row = lax.broadcasted_iota(jnp.int32, (tall, lanes), 0)
    begins = (row == HALO) | (row == HALO + local_y)
    ends = (row == HALO - 1) | (row == HALO + local_y - 1)

    def joined(p):
        get = lambda f, q=p, shift=0: got[GOT[f], q, y0 + shift:y3 + shift]
        b = buoy[p]
        stores = []
        if p < x3 - 1:
            more = -jnp.where(begins, get(SXY, p, -1), 0.0)
            if p in (x1 - 1, x2 - 1):
                more = more + get(SXX, p + 1)
            stores.append((state, (VX, p, rows), get(VX) + b * more))
        if p > 0:
            more_y = jnp.where(ends, get(SYY, p, 1), 0.0)
            more_z = -jnp.where(begins, get(SYZ, p, -1), 0.0)
            if p in (x1, x2):
                more_y = more_y - get(SXY, p - 1)
                more_z = more_z - get(SXZ, p - 1)
            stores.append((state, (VY, p, rows), get(VY) + b * more_y))
            stores.append((state, (VZ, p, rows), get(VZ) + b * more_z))
        return stores

    def load(f, p, low, high, shift=0):
        return state[f, p, low + shift:high + shift]

    def speeds(p):
        get = lambda f, q, shift=0: load(f, q, y0, y3, shift)
        q = p + 1
        sxy, sxz = get(SXY, p), get(SXZ, p)
        vx = get(VX, p) + buoy[p] * (
            get(SXX, q) - get(SXX, p) + (sxy - get(SXY, p, -1)) + behind_z(sxz))
        syz = get(SYZ, q)
        vy = get(VY, q) + buoy[q] * (
            get(SXY, q) - sxy + (get(SYY, q, 1) - get(SYY, q)) + behind_z(syz))
        vz = get(VZ, q) + buoy[q] * (
            get(SXZ, q) - sxz + (syz - get(SYZ, q, -1)) + ahead_z(get(SZZ, q)))
        return [(state, (VX, p, rows), vx), (state, (VY, q, rows), vy), (state, (VZ, q, rows), vz)]

    def stresses(first, last, p):
        a, b = (y1, y2) if last else (y0, y3)
        get = lambda f, q, shift=0: load(f, q, a, b, shift)
        old = (lambda f: got[GOT[f], p, a:b]) if first else (lambda f: load(f, p, a, b))
        part = slice(a - y0, b - y0)
        vx, vy, vz = get(VX, p), get(VY, p), get(VZ, p)
        lam, mu, kept = lame[p, part], shear[p, part], keep[p, part]
        exx, eyy, ezz = vx - get(VX, p - 1), vy - get(VY, p, -1), behind_z(vz)
        spread = lam * (exx + eyy + ezz)
        twice = 2.0 * mu
        new = {
            SXX: kept * old(SXX) + spread + twice * exx,
            SYY: kept * old(SYY) + spread + twice * eyy,
            SZZ: kept * old(SZZ) + spread + twice * ezz,
            SXY: kept * old(SXY) + mu * (get(VX, p, 1) - vx + (get(VY, p + 1) - vy)),
            SXZ: kept * old(SXZ) + mu * (ahead_z(vx) + (get(VZ, p + 1) - vz)),
            SYZ: kept * old(SYZ) + mu * (ahead_z(vy) + (get(VZ, p, 1) - vz)),
        }
        if last:
            new.update({VX: vx, VY: vy, VZ: vz})
            return [(out, (f, p - x1), value) for f, value in new.items()]
        return [(state, (f, p, rows), value) for f, value in new.items()]

    def each(body, first, after, pack=2):
        for p in range(first, after, pack):
            store([item for q in range(p, min(p + pack, after)) for item in body(q)])

    each(joined, x0, x3, 4)
    each(functools.partial(stresses, True, False), x0 + 1, x3 - 1)
    for done in range(1, STEPS):
        each(speeds, x0 + done, x3 - 2 - done + 1)
        each(functools.partial(stresses, False, done == STEPS - 1), x0 + 1 + done, x3 - 1 - done)

    def sent(there, *groups):
        pl.when(there)(lambda: wait_rows(sum(group.amount for group in groups), groups[0].send))

    for way in sides:
        sent(has["gy", way], labels_y[way], early[0, way], early[1, way], late[way])
        sent(has["gx", way], labels_x[way], faces[way])
        for k in range(2):
            sent(has["gy", -way] & has_x[k], corner_labels[k, way], corners[k, way])


def on_device(nx, ny, fields, labels, buoyancy, lame_first, shear_modulus, relax_rate):
    local_x, local_y, lanes = labels.shape
    wide = local_x + 2 * HALO
    tall = local_y + 2 * HALO
    padded = 2 * BASE + tall
    anywhere = pl.BlockSpec(memory_space=pl.ANY)
    table = pltpu.SMEM((LABELS,), jnp.float32)
    return pl.pallas_call(
        functools.partial(kernel, nx, ny),
        out_shape=pltpu.VMEM(fields.shape, jnp.float32),
        in_specs=[anywhere] * 6,
        out_specs=pl.BlockSpec(memory_space=pltpu.VMEM),
        scratch_shapes=[
            pltpu.VMEM((9, wide, padded, lanes), jnp.float32),
            pltpu.VMEM((9, wide, padded, lanes), jnp.float32),
            pltpu.VMEM((wide, padded, lanes), jnp.int32),
            pltpu.VMEM((wide, tall, lanes), jnp.float32),
            pltpu.VMEM((wide, tall, lanes), jnp.float32),
            pltpu.VMEM((wide, tall, lanes), jnp.float32),
            pltpu.VMEM((wide, tall, lanes), jnp.float32),
            pltpu.VMEM((6 * local_x * local_y, lanes), jnp.float32),
            table, table, table, table,
            pltpu.SemaphoreType.DMA((8,)),
            pltpu.SemaphoreType.DMA((20,)),
            pltpu.SemaphoreType.DMA((7,)),
        ],
        compiler_params=pltpu.CompilerParams(collective_id=0, has_side_effects=True),
        name="waves",
    )(fields, labels, buoyancy, lame_first, shear_modulus, relax_rate)


def solution(mesh):
    placed = (P(None, "gx", "gy", None), P("gx", "gy", None), P(), P(), P(), P())
    return jax.shard_map(
        functools.partial(on_device, mesh.shape["gx"], mesh.shape["gy"]),
        mesh=mesh, in_specs=placed, out_specs=P(None, "gx", "gy", None), check_vma=False,
    )
```

```python
import functools

import jax
import jax.numpy as jnp
from jax import lax
from jax.experimental import pallas as pl
from jax.experimental.pallas import tpu as pltpu
from jax.sharding import PartitionSpec as P

STEPS = 4
LABELS = 8
HALO = STEPS
BASE = 8
MESH = pl.DeviceIdType.MESH
VX, VY, VZ, SXX, SYY, SZZ, SXY, SXZ, SYZ = range(9)
GOT = (0, 2, 1, 6, 3, 7, 4, 8, 5)


def kernel(nx, ny, shape, fields, labels, buoy_h, lame_h, shear_h, relax_h, out, flat, flat_labels, got, vel, sig,
           tissue, buoy, lame, shear, keep, count, buoy_t, lame_t, shear_t, relax_t, send_sem, recv_sem, local_sem):
    local_x, local_y, lanes = shape
    block = local_x * local_y
    gx, gy = lax.axis_index("gx"), lax.axis_index("gy")
    has = {("gx", -1): gx > 0, ("gx", 1): gx < nx - 1, ("gy", -1): gy > 0, ("gy", 1): gy < ny - 1}
    place = {"gx": gx, "gy": gy}
    x0, x1, x2, x3 = BASE, BASE + HALO, BASE + HALO + local_x, BASE + local_x + 2 * HALO
    y0, y1, y2, y3 = 0, HALO, HALO + local_y, local_y + 2 * HALO
    whole, mine = (x0, x3), (x1, x2)

    barrier = pltpu.get_barrier_semaphore()
    for (axis, way), there in has.items():
        @pl.when(there)
        def _(axis=axis, way=way):
            pl.semaphore_signal(barrier, inc=1, device_id={axis: place[axis] + way}, device_id_type=MESH)

    copies = [pltpu.make_async_copy(source, target, local_sem.at[index]) for index, (source, target) in enumerate((
        (labels, flat_labels), (buoy_h, buoy_t), (fields, flat), (lame_h, lame_t), (shear_h, shear_t),
        (relax_h, relax_t)))]
    for copy in copies:
        copy.start()

    def wait_rows(amount, sem):
        pltpu.make_async_copy(count.at[:amount], count.at[:amount], sem).wait()

    def blank(a, b, c, d):
        got[:, c:d, a:b] = jnp.zeros((9, d - c, b - a, lanes), jnp.float32)
        tissue[c:d, a:b] = jnp.full((d - c, b - a, lanes), LABELS, jnp.int32)

    pl.when(jnp.logical_not(has["gx", -1]))(lambda: blank(x0, x1, y0, y3))
    pl.when(jnp.logical_not(has["gx", 1]))(lambda: blank(x2, x3, y0, y3))
    pl.when(jnp.logical_not(has["gy", -1]))(lambda: blank(x0, x3, y0, y1))
    pl.when(jnp.logical_not(has["gy", 1]))(lambda: blank(x0, x3, y2, y3))

    lane = lax.broadcasted_iota(jnp.int32, (x3 - x0, lanes), 1)
    first_z, last_z = lane == 0, lane == lanes - 1

    def ahead_z(a):
        following = pltpu.roll(a, lanes - 1, 1)
        return jnp.where(last_z[:a.shape[0]], 0.0, following) - a

    def behind_z(a):
        return a - jnp.where(first_z[:a.shape[0]], 0.0, pltpu.roll(a, 1, 1))

    cell = lax.broadcasted_iota(jnp.int32, (local_x, lanes), 0)
    first_x, last_x = cell == 0, cell == local_x - 1
    copies[0].wait()
    copies[1].wait()
    own_labels = []
    for y in range(local_y):
        label = flat_labels[pl.ds(y, local_x, stride=local_y), :]
        tissue[y1 + y, x1:x2] = label
        table = jnp.zeros(label.shape, jnp.float32)
        for kind in range(LABELS):
            table = jnp.where(label == kind, buoy_t[kind], table)
        buoy[y1 + y, x1 - x0:x2 - x0] = table
    copies[2].wait()

    def alone(y):
        get = lambda f, row=y: flat[pl.ds(f * block + row, local_x, stride=local_y), :]
        b = buoy[y1 + y, x1 - x0:x2 - x0]
        sxx, syy, szz, sxy, sxz, syz = (get(f) for f in range(SXX, SYZ + 1))
        xx = jnp.where(last_x, 0.0, pltpu.roll(sxx, local_x - 1, 0)) - sxx
        xy = sxy - jnp.where(first_x, 0.0, pltpu.roll(sxy, 1, 0))
        xz = sxz - jnp.where(first_x, 0.0, pltpu.roll(sxz, 1, 0))
        yx, yz = (sxy - get(SXY, y - 1), syz - get(SYZ, y - 1)) if y > 0 else (sxy, syz)
        yy = get(SYY, y + 1) - syy if y < local_y - 1 else -syy
        new = {
            VX: get(VX) + b * (xx + yx + behind_z(sxz)),
            VY: get(VY) + b * (xy + yy + behind_z(syz)),
            VZ: get(VZ) + b * (xz + yz + ahead_z(szz)),
            SXX: sxx, SYY: syy, SZZ: szz, SXY: sxy, SXZ: sxz, SYZ: syz,
        }
        return [(got, (GOT[f], y1 + y, slice(x1, x2)), value) for f, value in new.items()]

    def each(body, places, pack=2):
        places = list(places)
        for index in range(0, len(places), pack):
            for ref, where, value in [item for y in places[index:index + pack] for item in body(y)]:
                ref[where] = value

    each(alone, range(local_y))
    for copy in copies[3:]:
        copy.wait()
    pl.semaphore_wait(barrier, sum(there.astype(jnp.int32) for there in has.values()))

    odd = lax.rem(gx, 2) == 1
    ways = (jnp.where(odd, 1, -1), jnp.where(odd, -1, 1))
    has_x = (jnp.where(odd, gx < nx - 1, gx > 0), jnp.where(odd, gx > 0, gx < nx - 1))

    class Group:
        def __init__(self, send, recv):
            self.send, self.recv, self.copies, self.amount = send_sem.at[send], recv_sem.at[recv], [], 0

        def add(self, source, target, axis, way):
            size = 1
            for extent in source.shape[:-1]:
                size *= extent
            self.amount += size
            self.copies.append(pltpu.make_async_remote_copy(
                src_ref=source, dst_ref=target, send_sem=self.send, recv_sem=self.recv,
                device_id={axis: place[axis] + way}, device_id_type=MESH))
            return self

        def start(self, there):
            @pl.when(there)
            def _():
                for copy in self.copies:
                    copy.start()

        def arrive(self, there):
            pl.when(there)(lambda: wait_rows(self.amount, self.recv))

    def out_rows(way, near, far):
        return slice(y2 - far, y2 - near) if way == 1 else slice(y1 + near, y1 + far)

    def in_rows(way, near, far):
        return slice(y1 - far, y1 - near) if way == 1 else slice(y2 + near, y2 + far)

    def out_planes(way, near, far):
        return pl.ds(jnp.where(way == 1, x2 - far, x1 + near), far - near)

    def in_planes(way, near, far):
        return pl.ds(jnp.where(way == 1, x1 - far, x2 + near), far - near)

    def over_y(group, way, fs, planes, near, far):
        a, b = out_rows(way, near, far), in_rows(way, near, far)
        group.add(got.at[fs, a, planes], got.at[fs, b, planes], "gy", way)

    sides = (-1, 1)
    everything = slice(0, 9)
    labels_y, labels_x, early, late, faces, corner_labels, corners = {}, {}, {}, {}, {}, {}, {}
    for s, way in enumerate(sides):
        labels_y[way] = Group(s, s).add(
            tissue.at[out_rows(way, 0, HALO), x1:x2], tissue.at[in_rows(way, 0, HALO), x1:x2], "gy", way)
        a, b = (x2 - HALO, x1 - HALO) if way == 1 else (x1, x2)
        labels_x[way] = Group(2 + s, 2 + s).add(
            tissue.at[y1:y2, a:a + HALO], tissue.at[y1:y2, b:b + HALO], "gx", way)
        late[way] = Group(s, 4 + s)
        over_y(late[way], way, slice(0, 6) if way == 1 else everything, slice(x1 + 1, x2 - 1), 2, 3)
        over_y(late[way], way, slice(2, 3) if way == 1 else slice(0, 2), slice(x1, x2), 3, 4)
        over_y(late[way], way, everything, out_planes(ways[0], 2, 4), 1, 2)
        faces[way] = Group(2 + s, 6 + s)
        for fs, near, far in ((everything, 0, 3), (slice(0, 1) if way == 1 else slice(1, 3), 3, 4)):
            a, b = (x2 - far, x1 - far) if way == 1 else (x1 + near, x2 + near)
            faces[way].add(got.at[fs, y1:y2, a:a + far - near], got.at[fs, y1:y2, b:b + far - near], "gx", way)
        for k, x_way in enumerate(ways):
            tall = pl.ds(GOT[SXY] if way == 1 else jnp.where(x_way == 1, GOT[SXZ], GOT[SXX]), 1)
            parts = [(everything, 0, 1, 0, 3), (tall, 0, 1, 3, 4)]
            if k == 0:
                wide = pl.ds(jnp.where(x_way == 1, GOT[SXY], GOT[SYZ]) if way == 1 else GOT[SYY], 1)
                parts += [(everything, 1, 2, 0, 2), (everything, 2, 3, 0, 1), (wide, 3, 4, 0, 1)]
            else:
                parts += [(everything, 1, 4, 0, 2)]
            early[k, way] = Group(s, 8 + 2 * k + s)
            corner_labels[k, way] = Group(4 + 2 * k + s, 12 + 2 * k + s).add(
                tissue.at[in_rows(way, 0, 3), out_planes(x_way, 0, 3)],
                tissue.at[in_rows(way, 0, 3), in_planes(x_way, 0, 3)], "gx", x_way)
            corners[k, way] = Group(4 + 2 * k + s, 16 + 2 * k + s)
            for fs, x_near, x_far, near, far in parts:
                over_y(early[k, way], way, everything if x_near == 3 else fs, out_planes(x_way, x_near, x_far), near, far)
                corners[k, way].add(
                    got.at[fs, in_rows(way, near, far), out_planes(x_way, x_near, x_far)],
                    got.at[fs, in_rows(way, near, far), in_planes(x_way, x_near, x_far)], "gx", x_way)

    for way in sides:
        labels_y[way].start(has["gy", way])
    urgent = has_x[0]
    for way in sides:
        early[0, way].start(has["gy", way] & urgent)
    for way in sides:
        early[1, way].start(has["gy", way])
    for way in sides:
        early[0, way].start(has["gy", way] & jnp.logical_not(urgent))
    for way in sides:
        labels_x[way].start(has["gx", way])
    for way in sides:
        faces[way].start(has["gx", way])
    for way in sides:
        late[way].start(has["gy", way])

    for way in sides:
        labels_y[way].arrive(has["gy", -way])
        for k in range(2):
            corner_labels[k, way].start(has["gy", -way] & has_x[k])
    for k in range(2):
        for way in sides:
            early[k, way].arrive(has["gy", -way] & has_x[k])
            corners[k, way].start(has["gy", -way] & has_x[k])
    def look_up(first, after):
        @pl.loop(first, after)
        def _(row):
            label = tissue[row, x0:x3]
            tables = [jnp.zeros(label.shape, jnp.float32) for _ in range(4)]
            for kind in range(LABELS):
                here = label == kind
                values = (buoy_t[kind], lame_t[kind], shear_t[kind], 1.0 - relax_t[kind])
                tables = [jnp.where(here, value, old) for value, old in zip(values, tables)]
            for ref, table in zip((buoy, lame, shear, keep), tables):
                ref[row] = table

    def v(k, c, y, move=0, span=whole):
        return vel[3 * (k - 1) + c, y1 + y, span[0] + move:span[1] + move]

    def s(k, f, y, move=0, span=whole):
        part = slice(span[0] + move, span[1] + move)
        return sig[6 * (k - 1) + f - SXX, y1 + y, part] if k else got[GOT[f], y1 + y, part]

    def table(ref, y, span=whole):
        return ref[y1 + y, span[0] - x0:span[1] - x0]

    position = lax.broadcasted_iota(jnp.int32, (x3 - x0, lanes), 0)
    begins = (position == HALO) | (position == HALO + local_x)
    ends = (position == HALO - 1) | (position == HALO + local_x - 1)

    def speed_x(k, y):
        b = table(buoy, y)
        if k == 1:
            more = jnp.where(ends, s(0, SXX, y, 1), 0.0)
            if y in (0, local_y):
                more = more - s(0, SXY, y - 1)
            new = got[GOT[VX], y1 + y, x0:x3] + b * more
        else:
            new = v(k - 1, VX, y) + b * (
                s(k - 1, SXX, y, 1) - s(k - 1, SXX, y) + (s(k - 1, SXY, y) - s(k - 1, SXY, y - 1))
                + behind_z(s(k - 1, SXZ, y)))
        return [(vel, (3 * (k - 1) + VX, y1 + y, slice(x0, x3)), new)]

    def speed_y(k, y):
        b = table(buoy, y)
        if k == 1:
            more = -jnp.where(begins, s(0, SXY, y, -1), 0.0)
            if y in (-1, local_y - 1):
                more = more + s(0, SYY, y + 1)
            new = got[GOT[VY], y1 + y, x0:x3] + b * more
        else:
            new = v(k - 1, VY, y) + b * (
                s(k - 1, SXY, y) - s(k - 1, SXY, y, -1) + (s(k - 1, SYY, y + 1) - s(k - 1, SYY, y))
                + behind_z(s(k - 1, SYZ, y)))
        return [(vel, (3 * (k - 1) + VY, y1 + y, slice(x0, x3)), new)]

    def speed_z(k, y):
        b = table(buoy, y)
        if k == 1:
            more = -jnp.where(begins, s(0, SXZ, y, -1), 0.0)
            if y in (0, local_y):
                more = more - s(0, SYZ, y - 1)
            new = got[GOT[VZ], y1 + y, x0:x3] + b * more
        else:
            new = v(k - 1, VZ, y) + b * (
                s(k - 1, SXZ, y) - s(k - 1, SXZ, y, -1) + (s(k - 1, SYZ, y) - s(k - 1, SYZ, y - 1))
                + ahead_z(s(k - 1, SZZ, y)))
        return [(vel, (3 * (k - 1) + VZ, y1 + y, slice(x0, x3)), new)]

    def stresses(k, y):
        span = mine if k == STEPS else whole
        get = lambda c, row=y, move=0: v(k, c, row, move, span)
        old = lambda f: s(k - 1, f, y, 0, span)
        vx, vy, vz = get(VX), get(VY), get(VZ)
        lam, mu, kept = table(lame, y, span), table(shear, y, span), table(keep, y, span)
        exx, eyy, ezz = vx - get(VX, y, -1), vy - get(VY, y - 1), behind_z(vz)
        spread = lam * (exx + eyy + ezz)
        twice = 2.0 * mu
        new = {
            SXX: kept * old(SXX) + spread + twice * exx,
            SYY: kept * old(SYY) + spread + twice * eyy,
            SZZ: kept * old(SZZ) + spread + twice * ezz,
            SXY: kept * old(SXY) + mu * (get(VX, y + 1) - vx + (get(VY, y, 1) - vy)),
            SXZ: kept * old(SXZ) + mu * (ahead_z(vx) + (get(VZ, y, 1) - vz)),
            SYZ: kept * old(SYZ) + mu * (ahead_z(vy) + (get(VZ, y + 1) - vz)),
        }
        if k == STEPS:
            new.update({VX: vx, VY: vy, VZ: vz})
            return [(out, (pl.ds(f * block + y, local_x, stride=local_y), slice(None)), value)
                    for f, value in new.items()]
        return [(sig, (6 * (k - 1) + f - SXX, y1 + y, slice(x0, x3)), value) for f, value in new.items()]

    def reach(k, low, high, inner):
        known = range(k + low, local_y - k + high)
        if inner:
            return known
        needed = range(k - STEPS + low, local_y + STEPS - k + high)
        return [y for y in needed if y not in known]

    def steps(inner):
        for k in range(1, STEPS + 1):
            each(functools.partial(speed_x, k), reach(k, 0, 1, inner))
            each(functools.partial(speed_z, k), reach(k, 0, 1, inner))
            each(functools.partial(speed_y, k), reach(k, -1, 0, inner))
            each(functools.partial(stresses, k), reach(k, 0, 0, inner))

    for way in sides:
        labels_x[way].arrive(has["gx", -way])
    look_up(y1, y2)
    for way in sides:
        faces[way].arrive(has["gx", -way])
    steps(True)
    for k in range(2):
        for way in sides:
            corner_labels[k, way].arrive(has["gy", -way] & has_x[k])
    look_up(y0, y1)
    look_up(y2, y3)
    for way in sides:
        late[way].arrive(has["gy", -way])
        for k in range(2):
            early[k, way].arrive(has["gy", -way] & jnp.logical_not(has_x[k]))
    for k in range(2):
        for way in sides:
            corners[k, way].arrive(has["gy", -way] & has_x[k])
    steps(False)

    def sent(there, *groups):
        pl.when(there)(lambda: wait_rows(sum(group.amount for group in groups), groups[0].send))

    for way in sides:
        sent(has["gy", way], labels_y[way], early[0, way], early[1, way], late[way])
        sent(has["gx", way], labels_x[way], faces[way])
        for k in range(2):
            sent(has["gy", -way] & has_x[k], corner_labels[k, way], corners[k, way])


def on_device(nx, ny, fields, labels, buoyancy, lame_first, shear_modulus, relax_rate):
    local_x, local_y, lanes = labels.shape
    block = local_x * local_y
    wide = 2 * BASE + local_x + 2 * HALO
    tall = local_y + 2 * HALO
    anywhere = pl.BlockSpec(memory_space=pl.ANY)
    table = pltpu.SMEM((LABELS,), jnp.float32)
    moduli = pltpu.VMEM((tall, local_x + 2 * HALO, lanes), jnp.float32)
    advanced = pl.pallas_call(
        functools.partial(kernel, nx, ny, labels.shape),
        out_shape=pltpu.VMEM((9 * block, lanes), jnp.float32),
        in_specs=[anywhere] * 6,
        out_specs=pl.BlockSpec(memory_space=pltpu.VMEM),
        scratch_shapes=[
            pltpu.VMEM((9 * block, lanes), jnp.float32),
            pltpu.VMEM((block, lanes), jnp.int32),
            pltpu.VMEM((9, tall, wide, lanes), jnp.float32),
            pltpu.VMEM((3 * STEPS, tall, wide, lanes), jnp.float32),
            pltpu.VMEM((6 * STEPS - 6, tall, wide, lanes), jnp.float32),
            pltpu.VMEM((tall, wide, lanes), jnp.int32),
            moduli, moduli, moduli, moduli,
            pltpu.VMEM((6 * block, lanes), jnp.float32),
            table, table, table, table,
            pltpu.SemaphoreType.DMA((8,)),
            pltpu.SemaphoreType.DMA((20,)),
            pltpu.SemaphoreType.DMA((6,)),
        ],
        compiler_params=pltpu.CompilerParams(collective_id=0, has_side_effects=True),
        name="waves",
    )(fields.reshape(9 * block, lanes), labels.reshape(block, lanes), buoyancy, lame_first, shear_modulus, relax_rate)
    return advanced.reshape(fields.shape)


def solution(mesh):
    placed = (P(None, "gx", "gy", None), P("gx", "gy", None), P(), P(), P(), P())
    return jax.shard_map(
        functools.partial(on_device, mesh.shape["gx"], mesh.shape["gy"]),
        mesh=mesh, in_specs=placed, out_specs=P(None, "gx", "gy", None), check_vma=False,
    )
```

```python
import functools

import jax
import jax.numpy as jnp
from jax import lax
from jax.experimental import pallas as pl
from jax.experimental.pallas import tpu as pltpu
from jax.sharding import PartitionSpec as P

STEPS = 4
LABELS = 8
HALO = STEPS
BASE = 8
MESH = pl.DeviceIdType.MESH
VX, VY, VZ, SXX, SYY, SZZ, SXY, SXZ, SYZ = range(9)
GOT = (0, 2, 1, 6, 3, 7, 4, 8, 5)


def kernel(nx, ny, shape, fields, labels, buoy_h, lame_h, shear_h, relax_h, out, flat, flat_labels, got, vel, sig,
           tissue, buoy, lame, shear, keep, count, buoy_t, lame_t, shear_t, relax_t, send_sem, recv_sem, local_sem):
    local_x, local_y, lanes = shape
    block = local_x * local_y
    gx, gy = lax.axis_index("gx"), lax.axis_index("gy")
    has = {("gx", -1): gx > 0, ("gx", 1): gx < nx - 1, ("gy", -1): gy > 0, ("gy", 1): gy < ny - 1}
    place = {"gx": gx, "gy": gy}
    x0, x1, x2, x3 = BASE, BASE + HALO, BASE + HALO + local_x, BASE + local_x + 2 * HALO
    y0, y1, y2, y3 = 0, HALO, HALO + local_y, local_y + 2 * HALO
    whole, mine = (x0, x3), (x1, x2)

    barrier = pltpu.get_barrier_semaphore()
    for (axis, way), there in has.items():
        @pl.when(there)
        def _(axis=axis, way=way):
            pl.semaphore_signal(barrier, inc=1, device_id={axis: place[axis] + way}, device_id_type=MESH)

    copies = [pltpu.make_async_copy(source, target, local_sem.at[index]) for index, (source, target) in enumerate((
        (labels, flat_labels), (buoy_h, buoy_t), (fields, flat), (lame_h, lame_t), (shear_h, shear_t),
        (relax_h, relax_t)))]
    for copy in copies:
        copy.start()

    def wait_rows(amount, sem):
        pltpu.make_async_copy(count.at[:amount], count.at[:amount], sem).wait()

    def blank(a, b, c, d):
        got[:, c:d, a:b] = jnp.zeros((9, d - c, b - a, lanes), jnp.float32)
        tissue[c:d, a:b] = jnp.full((d - c, b - a, lanes), LABELS, jnp.int32)

    pl.when(jnp.logical_not(has["gx", -1]))(lambda: blank(x0, x1, y0, y3))
    pl.when(jnp.logical_not(has["gx", 1]))(lambda: blank(x2, x3, y0, y3))
    pl.when(jnp.logical_not(has["gy", -1]))(lambda: blank(x0, x3, y0, y1))
    pl.when(jnp.logical_not(has["gy", 1]))(lambda: blank(x0, x3, y2, y3))

    lane = lax.broadcasted_iota(jnp.int32, (x3 - x0, lanes), 1)
    first_z, last_z = lane == 0, lane == lanes - 1

    def ahead_z(a):
        following = pltpu.roll(a, lanes - 1, 1)
        return jnp.where(last_z[:a.shape[0]], 0.0, following) - a

    def behind_z(a):
        return a - jnp.where(first_z[:a.shape[0]], 0.0, pltpu.roll(a, 1, 1))

    cell = lax.broadcasted_iota(jnp.int32, (local_x, lanes), 0)
    first_x, last_x = cell == 0, cell == local_x - 1
    copies[0].wait()
    copies[1].wait()
    own_labels = []
    for y in range(local_y):
        label = flat_labels[pl.ds(y, local_x, stride=local_y), :]
        tissue[y1 + y, x1:x2] = label
        table = jnp.zeros(label.shape, jnp.float32)
        for kind in range(LABELS):
            table = jnp.where(label == kind, buoy_t[kind], table)
        buoy[y1 + y, x1 - x0:x2 - x0] = table
    copies[2].wait()

    def alone(y):
        get = lambda f, row=y: flat[pl.ds(f * block + row, local_x, stride=local_y), :]
        b = buoy[y1 + y, x1 - x0:x2 - x0]
        sxx, syy, szz, sxy, sxz, syz = (get(f) for f in range(SXX, SYZ + 1))
        xx = jnp.where(last_x, 0.0, pltpu.roll(sxx, local_x - 1, 0)) - sxx
        xy = sxy - jnp.where(first_x, 0.0, pltpu.roll(sxy, 1, 0))
        xz = sxz - jnp.where(first_x, 0.0, pltpu.roll(sxz, 1, 0))
        yx, yz = (sxy - get(SXY, y - 1), syz - get(SYZ, y - 1)) if y > 0 else (sxy, syz)
        yy = get(SYY, y + 1) - syy if y < local_y - 1 else -syy
        new = {
            VX: get(VX) + b * (xx + yx + behind_z(sxz)),
            VY: get(VY) + b * (xy + yy + behind_z(syz)),
            VZ: get(VZ) + b * (xz + yz + ahead_z(szz)),
            SXX: sxx, SYY: syy, SZZ: szz, SXY: sxy, SXZ: sxz, SYZ: syz,
        }
        return [(got, (GOT[f], y1 + y, slice(x1, x2)), value) for f, value in new.items()]

    def each(body, places, pack=2):
        places = list(places)
        for index in range(0, len(places), pack):
            for ref, where, value in [item for y in places[index:index + pack] for item in body(y)]:
                ref[where] = value

    each(alone, range(local_y))
    for copy in copies[3:]:
        copy.wait()
    pl.semaphore_wait(barrier, sum(there.astype(jnp.int32) for there in has.values()))

    odd = lax.rem(gx, 2) == 1
    ways = (jnp.where(odd, 1, -1), jnp.where(odd, -1, 1))
    has_x = (jnp.where(odd, gx < nx - 1, gx > 0), jnp.where(odd, gx > 0, gx < nx - 1))

    class Group:
        def __init__(self, send, recv):
            self.send, self.recv, self.copies, self.amount = send_sem.at[send], recv_sem.at[recv], [], 0

        def add(self, source, target, axis, way):
            size = 1
            for extent in source.shape[:-1]:
                size *= extent
            self.amount += size
            self.copies.append(pltpu.make_async_remote_copy(
                src_ref=source, dst_ref=target, send_sem=self.send, recv_sem=self.recv,
                device_id={axis: place[axis] + way}, device_id_type=MESH))
            return self

        def start(self, there):
            @pl.when(there)
            def _():
                for copy in self.copies:
                    copy.start()

        def arrive(self, there):
            pl.when(there)(lambda: wait_rows(self.amount, self.recv))

    def out_rows(way, near, far):
        return slice(y2 - far, y2 - near) if way == 1 else slice(y1 + near, y1 + far)

    def in_rows(way, near, far):
        return slice(y1 - far, y1 - near) if way == 1 else slice(y2 + near, y2 + far)

    def out_planes(way, near, far):
        return pl.ds(jnp.where(way == 1, x2 - far, x1 + near), far - near)

    def in_planes(way, near, far):
        return pl.ds(jnp.where(way == 1, x1 - far, x2 + near), far - near)

    def over_y(group, way, fs, planes, near, far):
        a, b = out_rows(way, near, far), in_rows(way, near, far)
        group.add(got.at[fs, a, planes], got.at[fs, b, planes], "gy", way)

    sides = (-1, 1)
    everything = slice(0, 9)
    labels_y, labels_x, early, late, faces, corner_labels, corners = {}, {}, {}, {}, {}, {}, {}
    for s, way in enumerate(sides):
        labels_y[way] = Group(s, s).add(
            tissue.at[out_rows(way, 0, HALO), x1:x2], tissue.at[in_rows(way, 0, HALO), x1:x2], "gy", way)
        a, b = (x2 - HALO, x1 - HALO) if way == 1 else (x1, x2)
        labels_x[way] = Group(2 + s, 2 + s).add(
            tissue.at[y1:y2, a:a + HALO], tissue.at[y1:y2, b:b + HALO], "gx", way)
        late[way] = Group(s, 4 + s)
        over_y(late[way], way, slice(0, 6) if way == 1 else everything, slice(x1 + 1, x2 - 1), 2, 3)
        over_y(late[way], way, slice(2, 3) if way == 1 else slice(0, 2), slice(x1, x2), 3, 4)
        over_y(late[way], way, everything, out_planes(ways[0], 2, 4), 1, 2)
        faces[way] = Group(2 + s, 6 + s)
        for fs, near, far in ((everything, 0, 3), (slice(0, 1) if way == 1 else slice(1, 3), 3, 4)):
            a, b = (x2 - far, x1 - far) if way == 1 else (x1 + near, x2 + near)
            faces[way].add(got.at[fs, y1:y2, a:a + far - near], got.at[fs, y1:y2, b:b + far - near], "gx", way)
        for k, x_way in enumerate(ways):
            tall = pl.ds(GOT[SXY] if way == 1 else jnp.where(x_way == 1, GOT[SXZ], GOT[SXX]), 1)
            parts = [(everything, 0, 1, 0, 3), (tall, 0, 1, 3, 4)]
            if k == 0:
                wide = pl.ds(jnp.where(x_way == 1, GOT[SXY], GOT[SYZ]) if way == 1 else GOT[SYY], 1)
                parts += [(everything, 1, 2, 0, 2), (everything, 2, 3, 0, 1), (wide, 3, 4, 0, 1)]
            else:
                parts += [(everything, 1, 4, 0, 2)]
            early[k, way] = Group(s, 8 + 2 * k + s)
            corner_labels[k, way] = Group(4 + 2 * k + s, 12 + 2 * k + s).add(
                tissue.at[in_rows(way, 0, 3), out_planes(x_way, 0, 3)],
                tissue.at[in_rows(way, 0, 3), in_planes(x_way, 0, 3)], "gx", x_way)
            corners[k, way] = Group(4 + 2 * k + s, 16 + 2 * k + s)
            for fs, x_near, x_far, near, far in parts:
                over_y(early[k, way], way, everything if x_near == 3 else fs, out_planes(x_way, x_near, x_far), near, far)
                corners[k, way].add(
                    got.at[fs, in_rows(way, near, far), out_planes(x_way, x_near, x_far)],
                    got.at[fs, in_rows(way, near, far), in_planes(x_way, x_near, x_far)], "gx", x_way)

    urgent = has_x[0]
    for way in sides:
        early[0, way].start(has["gy", way] & urgent)
    for way in sides:
        labels_y[way].start(has["gy", way])
    for way in sides:
        early[1, way].start(has["gy", way])
    for way in sides:
        early[0, way].start(has["gy", way] & jnp.logical_not(urgent))
    for way in sides:
        labels_x[way].start(has["gx", way])
    for way in sides:
        faces[way].start(has["gx", way])
    for way in sides:
        late[way].start(has["gy", way] & jnp.logical_not(urgent))

    for k in range(2):
        for way in sides:
            early[k, way].arrive(has["gy", -way] & has_x[k])
            corners[k, way].start(has["gy", -way] & has_x[k])
        if k == 0:
            for way in sides:
                late[way].start(has["gy", way] & urgent)
            for way in sides:
                labels_y[way].arrive(has["gy", -way])
                for j in range(2):
                    corner_labels[j, way].start(has["gy", -way] & has_x[j])
    def look_up(first, after):
        @pl.loop(first, after)
        def _(row):
            label = tissue[row, x0:x3]
            tables = [jnp.zeros(label.shape, jnp.float32) for _ in range(4)]
            for kind in range(LABELS):
                here = label == kind
                values = (buoy_t[kind], lame_t[kind], shear_t[kind], 1.0 - relax_t[kind])
                tables = [jnp.where(here, value, old) for value, old in zip(values, tables)]
            for ref, table in zip((buoy, lame, shear, keep), tables):
                ref[row] = table

    def v(k, c, y, move=0, span=whole):
        return vel[3 * (k - 1) + c, y1 + y, span[0] + move:span[1] + move]

    def s(k, f, y, move=0, span=whole):
        part = slice(span[0] + move, span[1] + move)
        return sig[6 * (k - 1) + f - SXX, y1 + y, part] if k else got[GOT[f], y1 + y, part]

    def table(ref, y, span=whole):
        return ref[y1 + y, span[0] - x0:span[1] - x0]

    position = lax.broadcasted_iota(jnp.int32, (x3 - x0, lanes), 0)
    begins = (position == HALO) | (position == HALO + local_x)
    ends = (position == HALO - 1) | (position == HALO + local_x - 1)

    def speed_x(k, y):
        b = table(buoy, y)
        if k == 1:
            more = jnp.where(ends, s(0, SXX, y, 1), 0.0)
            if y in (0, local_y):
                more = more - s(0, SXY, y - 1)
            new = got[GOT[VX], y1 + y, x0:x3] + b * more
        else:
            new = v(k - 1, VX, y) + b * (
                s(k - 1, SXX, y, 1) - s(k - 1, SXX, y) + (s(k - 1, SXY, y) - s(k - 1, SXY, y - 1))
                + behind_z(s(k - 1, SXZ, y)))
        return [(vel, (3 * (k - 1) + VX, y1 + y, slice(x0, x3)), new)]

    def speed_y(k, y):
        b = table(buoy, y)
        if k == 1:
            more = -jnp.where(begins, s(0, SXY, y, -1), 0.0)
            if y in (-1, local_y - 1):
                more = more + s(0, SYY, y + 1)
            new = got[GOT[VY], y1 + y, x0:x3] + b * more
        else:
            new = v(k - 1, VY, y) + b * (
                s(k - 1, SXY, y) - s(k - 1, SXY, y, -1) + (s(k - 1, SYY, y + 1) - s(k - 1, SYY, y))
                + behind_z(s(k - 1, SYZ, y)))
        return [(vel, (3 * (k - 1) + VY, y1 + y, slice(x0, x3)), new)]

    def speed_z(k, y):
        b = table(buoy, y)
        if k == 1:
            more = -jnp.where(begins, s(0, SXZ, y, -1), 0.0)
            if y in (0, local_y):
                more = more - s(0, SYZ, y - 1)
            new = got[GOT[VZ], y1 + y, x0:x3] + b * more
        else:
            new = v(k - 1, VZ, y) + b * (
                s(k - 1, SXZ, y) - s(k - 1, SXZ, y, -1) + (s(k - 1, SYZ, y) - s(k - 1, SYZ, y - 1))
                + ahead_z(s(k - 1, SZZ, y)))
        return [(vel, (3 * (k - 1) + VZ, y1 + y, slice(x0, x3)), new)]

    def stresses(k, y):
        span = mine if k == STEPS else whole
        get = lambda c, row=y, move=0: v(k, c, row, move, span)
        old = lambda f: s(k - 1, f, y, 0, span)
        vx, vy, vz = get(VX), get(VY), get(VZ)
        lam, mu, kept = table(lame, y, span), table(shear, y, span), table(keep, y, span)
        exx, eyy, ezz = vx - get(VX, y, -1), vy - get(VY, y - 1), behind_z(vz)
        spread = lam * (exx + eyy + ezz)
        twice = 2.0 * mu
        new = {
            SXX: kept * old(SXX) + spread + twice * exx,
            SYY: kept * old(SYY) + spread + twice * eyy,
            SZZ: kept * old(SZZ) + spread + twice * ezz,
            SXY: kept * old(SXY) + mu * (get(VX, y + 1) - vx + (get(VY, y, 1) - vy)),
            SXZ: kept * old(SXZ) + mu * (ahead_z(vx) + (get(VZ, y, 1) - vz)),
            SYZ: kept * old(SYZ) + mu * (ahead_z(vy) + (get(VZ, y + 1) - vz)),
        }
        if k == STEPS:
            new.update({VX: vx, VY: vy, VZ: vz})
            return [(out, (pl.ds(f * block + y, local_x, stride=local_y), slice(None)), value)
                    for f, value in new.items()]
        return [(sig, (6 * (k - 1) + f - SXX, y1 + y, slice(x0, x3)), value) for f, value in new.items()]

    def reach(k, low, high, inner):
        known = range(k + low, local_y - k + high)
        if inner:
            return known
        needed = range(k - STEPS + low, local_y + STEPS - k + high)
        return [y for y in needed if y not in known]

    def steps(inner):
        for k in range(1, STEPS + 1):
            each(functools.partial(speed_x, k), reach(k, 0, 1, inner))
            each(functools.partial(speed_z, k), reach(k, 0, 1, inner))
            each(functools.partial(speed_y, k), reach(k, -1, 0, inner))
            each(functools.partial(stresses, k), reach(k, 0, 0, inner))

    for way in sides:
        labels_x[way].arrive(has["gx", -way])
    look_up(y1, y2)
    for way in sides:
        faces[way].arrive(has["gx", -way])
    steps(True)
    for k in range(2):
        for way in sides:
            corner_labels[k, way].arrive(has["gy", -way] & has_x[k])
    look_up(y0, y1)
    look_up(y2, y3)
    for way in sides:
        late[way].arrive(has["gy", -way])
        for k in range(2):
            early[k, way].arrive(has["gy", -way] & jnp.logical_not(has_x[k]))
    for k in range(2):
        for way in sides:
            corners[k, way].arrive(has["gy", -way] & has_x[k])
    steps(False)

    def sent(there, *groups):
        pl.when(there)(lambda: wait_rows(sum(group.amount for group in groups), groups[0].send))

    for way in sides:
        sent(has["gy", way], labels_y[way], early[0, way], early[1, way], late[way])
        sent(has["gx", way], labels_x[way], faces[way])
        for k in range(2):
            sent(has["gy", -way] & has_x[k], corner_labels[k, way], corners[k, way])


def on_device(nx, ny, fields, labels, buoyancy, lame_first, shear_modulus, relax_rate):
    local_x, local_y, lanes = labels.shape
    block = local_x * local_y
    wide = 2 * BASE + local_x + 2 * HALO
    tall = local_y + 2 * HALO
    anywhere = pl.BlockSpec(memory_space=pl.ANY)
    table = pltpu.SMEM((LABELS,), jnp.float32)
    moduli = pltpu.VMEM((tall, local_x + 2 * HALO, lanes), jnp.float32)
    advanced = pl.pallas_call(
        functools.partial(kernel, nx, ny, labels.shape),
        out_shape=pltpu.VMEM((9 * block, lanes), jnp.float32),
        in_specs=[anywhere] * 6,
        out_specs=pl.BlockSpec(memory_space=pltpu.VMEM),
        scratch_shapes=[
            pltpu.VMEM((9 * block, lanes), jnp.float32),
            pltpu.VMEM((block, lanes), jnp.int32),
            pltpu.VMEM((9, tall, wide, lanes), jnp.float32),
            pltpu.VMEM((3 * STEPS, tall, wide, lanes), jnp.float32),
            pltpu.VMEM((6 * STEPS - 6, tall, wide, lanes), jnp.float32),
            pltpu.VMEM((tall, wide, lanes), jnp.int32),
            moduli, moduli, moduli, moduli,
            pltpu.VMEM((6 * block, lanes), jnp.float32),
            table, table, table, table,
            pltpu.SemaphoreType.DMA((8,)),
            pltpu.SemaphoreType.DMA((20,)),
            pltpu.SemaphoreType.DMA((6,)),
        ],
        compiler_params=pltpu.CompilerParams(collective_id=0, has_side_effects=True),
        name="waves",
    )(fields.reshape(9 * block, lanes), labels.reshape(block, lanes), buoyancy, lame_first, shear_modulus, relax_rate)
    return advanced.reshape(fields.shape)


def solution(mesh):
    placed = (P(None, "gx", "gy", None), P("gx", "gy", None), P(), P(), P(), P())
    return jax.shard_map(
        functools.partial(on_device, mesh.shape["gx"], mesh.shape["gy"]),
        mesh=mesh, in_specs=placed, out_specs=P(None, "gx", "gy", None), check_vma=False,
    )
```

```python
import functools

import jax
import jax.numpy as jnp
from jax import lax
from jax.experimental import pallas as pl
from jax.experimental.pallas import tpu as pltpu
from jax.sharding import PartitionSpec as P

STEPS = 4
LABELS = 8
HALO = STEPS
BASE = 8
MESH = pl.DeviceIdType.MESH
VX, VY, VZ, SXX, SYY, SZZ, SXY, SXZ, SYZ = range(9)
GOT = (0, 2, 1, 6, 3, 7, 4, 8, 5)


def kernel(nx, ny, shape, fields, labels, buoy_h, lame_h, shear_h, relax_h, out, flat, flat_labels, got, vel, sig,
           tissue, buoy, lame, shear, keep, count, buoy_t, lame_t, shear_t, relax_t, send_sem, recv_sem, local_sem):
    local_x, local_y, lanes = shape
    block = local_x * local_y
    gx, gy = lax.axis_index("gx"), lax.axis_index("gy")
    has = {("gx", -1): gx > 0, ("gx", 1): gx < nx - 1, ("gy", -1): gy > 0, ("gy", 1): gy < ny - 1}
    place = {"gx": gx, "gy": gy}
    x0, x1, x2, x3 = BASE, BASE + HALO, BASE + HALO + local_x, BASE + local_x + 2 * HALO
    y0, y1, y2, y3 = 0, HALO, HALO + local_y, local_y + 2 * HALO
    whole, mine = (x0, x3), (x1, x2)

    barrier = pltpu.get_barrier_semaphore()
    for (axis, way), there in has.items():
        @pl.when(there)
        def _(axis=axis, way=way):
            pl.semaphore_signal(barrier, inc=1, device_id={axis: place[axis] + way}, device_id_type=MESH)

    copies = [pltpu.make_async_copy(source, target, local_sem.at[index]) for index, (source, target) in enumerate((
        (labels, flat_labels), (buoy_h, buoy_t), (fields, flat), (lame_h, lame_t), (shear_h, shear_t),
        (relax_h, relax_t)))]
    for copy in copies:
        copy.start()

    def wait_rows(amount, sem):
        pltpu.make_async_copy(count.at[:amount], count.at[:amount], sem).wait()

    def blank(a, b, c, d):
        got[:, c:d, a:b] = jnp.zeros((9, d - c, b - a, lanes), jnp.float32)
        tissue[c:d, a:b] = jnp.full((d - c, b - a, lanes), LABELS, jnp.int32)

    pl.when(jnp.logical_not(has["gx", -1]))(lambda: blank(x0, x1, y0, y3))
    pl.when(jnp.logical_not(has["gx", 1]))(lambda: blank(x2, x3, y0, y3))
    pl.when(jnp.logical_not(has["gy", -1]))(lambda: blank(x0, x3, y0, y1))
    pl.when(jnp.logical_not(has["gy", 1]))(lambda: blank(x0, x3, y2, y3))

    lane = lax.broadcasted_iota(jnp.int32, (x3 - x0, lanes), 1)
    first_z, last_z = lane == 0, lane == lanes - 1

    def ahead_z(a):
        following = pltpu.roll(a, lanes - 1, 1)
        return jnp.where(last_z[:a.shape[0]], 0.0, following) - a

    def behind_z(a):
        return a - jnp.where(first_z[:a.shape[0]], 0.0, pltpu.roll(a, 1, 1))

    cell = lax.broadcasted_iota(jnp.int32, (local_x, lanes), 0)
    first_x, last_x = cell == 0, cell == local_x - 1
    copies[0].wait()
    copies[1].wait()
    own_labels = []
    for y in range(local_y):
        label = flat_labels[pl.ds(y, local_x, stride=local_y), :]
        tissue[y1 + y, x1:x2] = label
        table = jnp.zeros(label.shape, jnp.float32)
        for kind in range(LABELS):
            table = jnp.where(label == kind, buoy_t[kind], table)
        buoy[y1 + y, x1 - x0:x2 - x0] = table
    copies[2].wait()

    def alone(y):
        get = lambda f, row=y: flat[pl.ds(f * block + row, local_x, stride=local_y), :]
        b = buoy[y1 + y, x1 - x0:x2 - x0]
        sxx, syy, szz, sxy, sxz, syz = (get(f) for f in range(SXX, SYZ + 1))
        xx = jnp.where(last_x, 0.0, pltpu.roll(sxx, local_x - 1, 0)) - sxx
        xy = sxy - jnp.where(first_x, 0.0, pltpu.roll(sxy, 1, 0))
        xz = sxz - jnp.where(first_x, 0.0, pltpu.roll(sxz, 1, 0))
        yx, yz = (sxy - get(SXY, y - 1), syz - get(SYZ, y - 1)) if y > 0 else (sxy, syz)
        yy = get(SYY, y + 1) - syy if y < local_y - 1 else -syy
        new = {
            VX: get(VX) + b * (xx + yx + behind_z(sxz)),
            VY: get(VY) + b * (xy + yy + behind_z(syz)),
            VZ: get(VZ) + b * (xz + yz + ahead_z(szz)),
            SXX: sxx, SYY: syy, SZZ: szz, SXY: sxy, SXZ: sxz, SYZ: syz,
        }
        return [(got, (GOT[f], y1 + y, slice(x1, x2)), value) for f, value in new.items()]

    def each(body, places, pack=2):
        places = list(places)
        for index in range(0, len(places), pack):
            for ref, where, value in [item for y in places[index:index + pack] for item in body(y)]:
                ref[where] = value

    each(alone, range(local_y))
    for copy in copies[3:]:
        copy.wait()
    pl.semaphore_wait(barrier, sum(there.astype(jnp.int32) for there in has.values()))

    odd = lax.rem(gx, 2) == 1
    ways = (jnp.where(odd, 1, -1), jnp.where(odd, -1, 1))
    has_x = (jnp.where(odd, gx < nx - 1, gx > 0), jnp.where(odd, gx > 0, gx < nx - 1))

    class Group:
        def __init__(self, send, recv):
            self.send, self.recv, self.copies, self.amount = send_sem.at[send], recv_sem.at[recv], [], 0

        def add(self, source, target, axis, way):
            size = 1
            for extent in source.shape[:-1]:
                size *= extent
            self.amount += size
            self.copies.append(pltpu.make_async_remote_copy(
                src_ref=source, dst_ref=target, send_sem=self.send, recv_sem=self.recv,
                device_id={axis: place[axis] + way}, device_id_type=MESH))
            return self

        def start(self, there):
            @pl.when(there)
            def _():
                for copy in self.copies:
                    copy.start()

        def arrive(self, there):
            pl.when(there)(lambda: wait_rows(self.amount, self.recv))

    def out_rows(way, near, far):
        return slice(y2 - far, y2 - near) if way == 1 else slice(y1 + near, y1 + far)

    def in_rows(way, near, far):
        return slice(y1 - far, y1 - near) if way == 1 else slice(y2 + near, y2 + far)

    def out_planes(way, near, far):
        return pl.ds(jnp.where(way == 1, x2 - far, x1 + near), far - near)

    def in_planes(way, near, far):
        return pl.ds(jnp.where(way == 1, x1 - far, x2 + near), far - near)

    def over_y(group, way, fs, planes, near, far):
        a, b = out_rows(way, near, far), in_rows(way, near, far)
        group.add(got.at[fs, a, planes], got.at[fs, b, planes], "gy", way)

    sides = (-1, 1)
    everything = slice(0, 9)
    labels_y, labels_x, early, late, faces, corner_labels, corners = {}, {}, {}, {}, {}, {}, {}
    for s, way in enumerate(sides):
        labels_y[way] = Group(s, s).add(
            tissue.at[out_rows(way, 0, 3), x1:x2], tissue.at[in_rows(way, 0, 3), x1:x2], "gy", way)
        for a in (x1,) if way == 1 else (x1, x2 - 1):
            labels_y[way].add(tissue.at[out_rows(way, 3, 4), a:a + 1], tissue.at[in_rows(way, 3, 4), a:a + 1], "gy", way)
        a, b = (x2 - HALO, x1 - HALO) if way == 1 else (x1, x2)
        labels_x[way] = Group(2 + s, 2 + s).add(
            tissue.at[y1:y2, a:a + HALO], tissue.at[y1:y2, b:b + HALO], "gx", way)
        late[way] = Group(s, 4 + s)
        over_y(late[way], way, slice(0, 6) if way == 1 else everything, slice(x1 + 1, x2 - 1), 2, 3)
        over_y(late[way], way, slice(2, 3) if way == 1 else slice(0, 2), slice(x1, x2), 3, 4)
        over_y(late[way], way, everything, out_planes(ways[0], 2, 4), 1, 2)
        for fs in (slice(0, 4), slice(6, 9)) if way == 1 else (slice(0, 3), slice(4, 9)):
            over_y(late[way], way, fs, out_planes(ways[0], 3, 4), 0, 1)
        faces[way] = Group(2 + s, 6 + s)
        for fs, near, far in ((everything, 0, 3), (slice(0, 1) if way == 1 else slice(1, 3), 3, 4)):
            a, b = (x2 - far, x1 - far) if way == 1 else (x1 + near, x2 + near)
            faces[way].add(got.at[fs, y1:y2, a:a + far - near], got.at[fs, y1:y2, b:b + far - near], "gx", way)
        for k, x_way in enumerate(ways):
            tall = pl.ds(GOT[SXY] if way == 1 else jnp.where(x_way == 1, GOT[SXZ], GOT[SXX]), 1)
            parts = [(everything, 0, 1, 0, 3), (tall, 0, 1, 3, 4)]
            if k == 0:
                wide = pl.ds(jnp.where(x_way == 1, GOT[SXY], GOT[SYZ]) if way == 1 else GOT[SYY], 1)
                parts += [(everything, 1, 2, 0, 2), (everything, 2, 3, 0, 1), (wide, 3, 4, 0, 1)]
            else:
                parts += [(everything, 1, 4, 0, 2)]
            early[k, way] = Group(s, 8 + 2 * k + s)
            corner_labels[k, way] = Group(4 + 2 * k + s, 12 + 2 * k + s).add(
                tissue.at[in_rows(way, 0, 3), out_planes(x_way, 0, 3)],
                tissue.at[in_rows(way, 0, 3), in_planes(x_way, 0, 3)], "gx", x_way)
            corners[k, way] = Group(4 + 2 * k + s, 16 + 2 * k + s)
            for fs, x_near, x_far, near, far in parts:
                over_y(early[k, way], way, (slice(4, 6) if way == 1 else slice(3, 4)) if x_near == 3 else fs, out_planes(x_way, x_near, x_far), near, far)
                corners[k, way].add(
                    got.at[fs, in_rows(way, near, far), out_planes(x_way, x_near, x_far)],
                    got.at[fs, in_rows(way, near, far), in_planes(x_way, x_near, x_far)], "gx", x_way)

    urgent = has_x[0]
    calm = jnp.logical_not(urgent) & odd
    for way in sides:
        early[0, way].start(has["gy", way] & urgent)
    for way in sides:
        labels_y[way].start(has["gy", way])
    for way in sides:
        early[1, way].start(has["gy", way])
    for way in sides:
        early[0, way].start(has["gy", way] & jnp.logical_not(urgent | calm))
    for way in sides:
        labels_x[way].start(has["gx", way])
    for way in sides:
        faces[way].start(has["gx", way])
    for way in sides:
        late[way].start(has["gy", way] & jnp.logical_not(urgent | calm))

    for k in range(2):
        for way in sides:
            early[k, way].arrive(has["gy", -way] & has_x[k])
            corners[k, way].start(has["gy", -way] & has_x[k])
        if k == 0:
            for way in sides:
                late[way].start(has["gy", way] & urgent)
            for way in sides:
                labels_y[way].arrive(has["gy", -way])
                for j in range(2):
                    corner_labels[j, way].start(has["gy", -way] & has_x[j])
    for way in sides:
        early[0, way].start(has["gy", way] & calm)
        late[way].start(has["gy", way] & calm)

    def look_up(first, after):
        @pl.loop(first, after)
        def _(row):
            label = tissue[row, x0:x3]
            tables = [jnp.zeros(label.shape, jnp.float32) for _ in range(4)]
            for kind in range(LABELS):
                here = label == kind
                values = (buoy_t[kind], lame_t[kind], shear_t[kind], 1.0 - relax_t[kind])
                tables = [jnp.where(here, value, old) for value, old in zip(values, tables)]
            for ref, table in zip((buoy, lame, shear, keep), tables):
                ref[row] = table

    def v(k, c, y, move=0, span=whole):
        return vel[3 * (k - 1) + c, y1 + y, span[0] + move:span[1] + move]

    def s(k, f, y, move=0, span=whole):
        part = slice(span[0] + move, span[1] + move)
        return sig[6 * (k - 1) + f - SXX, y1 + y, part] if k else got[GOT[f], y1 + y, part]

    def table(ref, y, span=whole):
        return ref[y1 + y, span[0] - x0:span[1] - x0]

    position = lax.broadcasted_iota(jnp.int32, (x3 - x0, lanes), 0)
    begins = (position == HALO) | (position == HALO + local_x)
    ends = (position == HALO - 1) | (position == HALO + local_x - 1)

    def speed_x(k, y):
        b = table(buoy, y)
        if k == 1:
            more = jnp.where(ends, s(0, SXX, y, 1), 0.0)
            if y in (0, local_y):
                more = more - s(0, SXY, y - 1)
            new = got[GOT[VX], y1 + y, x0:x3] + b * more
        else:
            new = v(k - 1, VX, y) + b * (
                s(k - 1, SXX, y, 1) - s(k - 1, SXX, y) + (s(k - 1, SXY, y) - s(k - 1, SXY, y - 1))
                + behind_z(s(k - 1, SXZ, y)))
        return [(vel, (3 * (k - 1) + VX, y1 + y, slice(x0, x3)), new)]

    def speed_y(k, y):
        b = table(buoy, y)
        if k == 1:
            more = -jnp.where(begins, s(0, SXY, y, -1), 0.0)
            if y in (-1, local_y - 1):
                more = more + s(0, SYY, y + 1)
            new = got[GOT[VY], y1 + y, x0:x3] + b * more
        else:
            new = v(k - 1, VY, y) + b * (
                s(k - 1, SXY, y) - s(k - 1, SXY, y, -1) + (s(k - 1, SYY, y + 1) - s(k - 1, SYY, y))
                + behind_z(s(k - 1, SYZ, y)))
        return [(vel, (3 * (k - 1) + VY, y1 + y, slice(x0, x3)), new)]

    def speed_z(k, y):
        b = table(buoy, y)
        if k == 1:
            more = -jnp.where(begins, s(0, SXZ, y, -1), 0.0)
            if y in (0, local_y):
                more = more - s(0, SYZ, y - 1)
            new = got[GOT[VZ], y1 + y, x0:x3] + b * more
        else:
            new = v(k - 1, VZ, y) + b * (
                s(k - 1, SXZ, y) - s(k - 1, SXZ, y, -1) + (s(k - 1, SYZ, y) - s(k - 1, SYZ, y - 1))
                + ahead_z(s(k - 1, SZZ, y)))
        return [(vel, (3 * (k - 1) + VZ, y1 + y, slice(x0, x3)), new)]

    def stresses(k, y):
        span = mine if k == STEPS else whole
        get = lambda c, row=y, move=0: v(k, c, row, move, span)
        old = lambda f: s(k - 1, f, y, 0, span)
        vx, vy, vz = get(VX), get(VY), get(VZ)
        lam, mu, kept = table(lame, y, span), table(shear, y, span), table(keep, y, span)
        exx, eyy, ezz = vx - get(VX, y, -1), vy - get(VY, y - 1), behind_z(vz)
        spread = lam * (exx + eyy + ezz)
        twice = 2.0 * mu
        new = {
            SXX: kept * old(SXX) + spread + twice * exx,
            SYY: kept * old(SYY) + spread + twice * eyy,
            SZZ: kept * old(SZZ) + spread + twice * ezz,
            SXY: kept * old(SXY) + mu * (get(VX, y + 1) - vx + (get(VY, y, 1) - vy)),
            SXZ: kept * old(SXZ) + mu * (ahead_z(vx) + (get(VZ, y, 1) - vz)),
            SYZ: kept * old(SYZ) + mu * (ahead_z(vy) + (get(VZ, y + 1) - vz)),
        }
        if k == STEPS:
            new.update({VX: vx, VY: vy, VZ: vz})
            return [(out, (pl.ds(f * block + y, local_x, stride=local_y), slice(None)), value)
                    for f, value in new.items()]
        return [(sig, (6 * (k - 1) + f - SXX, y1 + y, slice(x0, x3)), value) for f, value in new.items()]

    def reach(k, low, high, inner):
        known = range(k + low, local_y - k + high)
        if inner:
            return known
        needed = range(k - STEPS + low, local_y + STEPS - k + high)
        return [y for y in needed if y not in known]

    def steps(inner):
        for k in range(1, STEPS + 1):
            each(functools.partial(speed_x, k), reach(k, 0, 1, inner))
            each(functools.partial(speed_z, k), reach(k, 0, 1, inner))
            each(functools.partial(speed_y, k), reach(k, -1, 0, inner))
            each(functools.partial(stresses, k), reach(k, 0, 0, inner))

    for way in sides:
        labels_x[way].arrive(has["gx", -way])
    look_up(y1, y2)
    for way in sides:
        faces[way].arrive(has["gx", -way])
    steps(True)
    for k in range(2):
        for way in sides:
            corner_labels[k, way].arrive(has["gy", -way] & has_x[k])
    look_up(y0, y1)
    look_up(y2, y3)
    for way in sides:
        late[way].arrive(has["gy", -way])
        for k in range(2):
            early[k, way].arrive(has["gy", -way] & jnp.logical_not(has_x[k]))
    for k in range(2):
        for way in sides:
            corners[k, way].arrive(has["gy", -way] & has_x[k])
    steps(False)

    def sent(there, *groups):
        pl.when(there)(lambda: wait_rows(sum(group.amount for group in groups), groups[0].send))

    for way in sides:
        sent(has["gy", way], labels_y[way], early[0, way], early[1, way], late[way])
        sent(has["gx", way], labels_x[way], faces[way])
        for k in range(2):
            sent(has["gy", -way] & has_x[k], corner_labels[k, way], corners[k, way])


def on_device(nx, ny, fields, labels, buoyancy, lame_first, shear_modulus, relax_rate):
    local_x, local_y, lanes = labels.shape
    block = local_x * local_y
    wide = 2 * BASE + local_x + 2 * HALO
    tall = local_y + 2 * HALO
    anywhere = pl.BlockSpec(memory_space=pl.ANY)
    table = pltpu.SMEM((LABELS,), jnp.float32)
    moduli = pltpu.VMEM((tall, local_x + 2 * HALO, lanes), jnp.float32)
    advanced = pl.pallas_call(
        functools.partial(kernel, nx, ny, labels.shape),
        out_shape=pltpu.VMEM((9 * block, lanes), jnp.float32),
        in_specs=[anywhere] * 6,
        out_specs=pl.BlockSpec(memory_space=pltpu.VMEM),
        scratch_shapes=[
            pltpu.VMEM((9 * block, lanes), jnp.float32),
            pltpu.VMEM((block, lanes), jnp.int32),
            pltpu.VMEM((9, tall, wide, lanes), jnp.float32),
            pltpu.VMEM((3 * STEPS, tall, wide, lanes), jnp.float32),
            pltpu.VMEM((6 * STEPS - 6, tall, wide, lanes), jnp.float32),
            pltpu.VMEM((tall, wide, lanes), jnp.int32),
            moduli, moduli, moduli, moduli,
            pltpu.VMEM((6 * block, lanes), jnp.float32),
            table, table, table, table,
            pltpu.SemaphoreType.DMA((8,)),
            pltpu.SemaphoreType.DMA((20,)),
            pltpu.SemaphoreType.DMA((6,)),
        ],
        compiler_params=pltpu.CompilerParams(collective_id=0, has_side_effects=True),
        name="waves",
    )(fields.reshape(9 * block, lanes), labels.reshape(block, lanes), buoyancy, lame_first, shear_modulus, relax_rate)
    return advanced.reshape(fields.shape)


def solution(mesh):
    placed = (P(None, "gx", "gy", None), P("gx", "gy", None), P(), P(), P(), P())
    return jax.shard_map(
        functools.partial(on_device, mesh.shape["gx"], mesh.shape["gy"]),
        mesh=mesh, in_specs=placed, out_specs=P(None, "gx", "gy", None), check_vma=False,
    )
```

```python
import functools

import jax
import jax.numpy as jnp
from jax import lax
from jax.experimental import pallas as pl
from jax.experimental.pallas import tpu as pltpu
from jax.sharding import PartitionSpec as P

STEPS = 4
LABELS = 8
HALO = STEPS
BASE = 8
MESH = pl.DeviceIdType.MESH
VX, VY, VZ, SXX, SYY, SZZ, SXY, SXZ, SYZ = range(9)
GOT = (0, 2, 1, 6, 3, 7, 4, 8, 5)


def kernel(nx, ny, shape, fields, labels, buoy_h, lame_h, shear_h, relax_h, out, flat, flat_labels, got, vel, sig,
           tissue, buoy, lame, shear, keep, count, buoy_t, lame_t, shear_t, relax_t, send_sem, recv_sem, local_sem):
    local_x, local_y, lanes = shape
    block = local_x * local_y
    gx, gy = lax.axis_index("gx"), lax.axis_index("gy")
    has = {("gx", -1): gx > 0, ("gx", 1): gx < nx - 1, ("gy", -1): gy > 0, ("gy", 1): gy < ny - 1}
    place = {"gx": gx, "gy": gy}
    x0, x1, x2, x3 = BASE, BASE + HALO, BASE + HALO + local_x, BASE + local_x + 2 * HALO
    y0, y1, y2, y3 = 0, HALO, HALO + local_y, local_y + 2 * HALO
    whole, mine = (x0, x3), (x1, x2)

    barrier = pltpu.get_barrier_semaphore()
    for (axis, way), there in has.items():
        @pl.when(there)
        def _(axis=axis, way=way):
            pl.semaphore_signal(barrier, inc=1, device_id={axis: place[axis] + way}, device_id_type=MESH)

    copies = [pltpu.make_async_copy(source, target, local_sem.at[index]) for index, (source, target) in enumerate((
        (labels, flat_labels), (buoy_h, buoy_t), (fields, flat), (lame_h, lame_t), (shear_h, shear_t),
        (relax_h, relax_t)))]
    for copy in copies:
        copy.start()

    def wait_rows(amount, sem):
        pltpu.make_async_copy(count.at[:amount], count.at[:amount], sem).wait()

    def blank(a, b, c, d):
        got[:, c:d, a:b] = jnp.zeros((9, d - c, b - a, lanes), jnp.float32)
        tissue[c:d, a:b] = jnp.full((d - c, b - a, lanes), LABELS, jnp.int32)

    pl.when(jnp.logical_not(has["gx", -1]))(lambda: blank(x0, x1, y0, y3))
    pl.when(jnp.logical_not(has["gx", 1]))(lambda: blank(x2, x3, y0, y3))
    pl.when(jnp.logical_not(has["gy", -1]))(lambda: blank(x0, x3, y0, y1))
    pl.when(jnp.logical_not(has["gy", 1]))(lambda: blank(x0, x3, y2, y3))

    lane = lax.broadcasted_iota(jnp.int32, (x3 - x0, lanes), 1)
    first_z, last_z = lane == 0, lane == lanes - 1

    def ahead_z(a):
        following = pltpu.roll(a, lanes - 1, 1)
        return jnp.where(last_z[:a.shape[0]], 0.0, following) - a

    def behind_z(a):
        return a - jnp.where(first_z[:a.shape[0]], 0.0, pltpu.roll(a, 1, 1))

    cell = lax.broadcasted_iota(jnp.int32, (local_x, lanes), 0)
    first_x, last_x = cell == 0, cell == local_x - 1
    copies[0].wait()
    copies[1].wait()
    own_labels = []
    for y in range(local_y):
        label = flat_labels[pl.ds(y, local_x, stride=local_y), :]
        tissue[y1 + y, x1:x2] = label
        table = jnp.zeros(label.shape, jnp.float32)
        for kind in range(LABELS):
            table = jnp.where(label == kind, buoy_t[kind], table)
        buoy[y1 + y, x1 - x0:x2 - x0] = table
    copies[2].wait()

    def alone(y):
        get = lambda f, row=y: flat[pl.ds(f * block + row, local_x, stride=local_y), :]
        b = buoy[y1 + y, x1 - x0:x2 - x0]
        sxx, syy, szz, sxy, sxz, syz = (get(f) for f in range(SXX, SYZ + 1))
        xx = jnp.where(last_x, 0.0, pltpu.roll(sxx, local_x - 1, 0)) - sxx
        xy = sxy - jnp.where(first_x, 0.0, pltpu.roll(sxy, 1, 0))
        xz = sxz - jnp.where(first_x, 0.0, pltpu.roll(sxz, 1, 0))
        yx, yz = (sxy - get(SXY, y - 1), syz - get(SYZ, y - 1)) if y > 0 else (sxy, syz)
        yy = get(SYY, y + 1) - syy if y < local_y - 1 else -syy
        new = {
            VX: get(VX) + b * (xx + yx + behind_z(sxz)),
            VY: get(VY) + b * (xy + yy + behind_z(syz)),
            VZ: get(VZ) + b * (xz + yz + ahead_z(szz)),
            SXX: sxx, SYY: syy, SZZ: szz, SXY: sxy, SXZ: sxz, SYZ: syz,
        }
        return [(got, (GOT[f], y1 + y, slice(x1, x2)), value) for f, value in new.items()]

    def each(body, places, pack=2):
        places = list(places)
        for index in range(0, len(places), pack):
            for ref, where, value in [item for y in places[index:index + pack] for item in body(y)]:
                ref[where] = value

    each(alone, range(local_y))
    for copy in copies[3:]:
        copy.wait()
    pl.semaphore_wait(barrier, sum(there.astype(jnp.int32) for there in has.values()))

    odd = lax.rem(gx, 2) == 1
    ways = (jnp.where(odd, 1, -1), jnp.where(odd, -1, 1))
    has_x = (jnp.where(odd, gx < nx - 1, gx > 0), jnp.where(odd, gx > 0, gx < nx - 1))

    class Group:
        def __init__(self, send, recv):
            self.send, self.recv, self.copies, self.amount = send_sem.at[send], recv_sem.at[recv], [], 0

        def add(self, source, target, axis, way):
            size = 1
            for extent in source.shape[:-1]:
                size *= extent
            self.amount += size
            self.copies.append(pltpu.make_async_remote_copy(
                src_ref=source, dst_ref=target, send_sem=self.send, recv_sem=self.recv,
                device_id={axis: place[axis] + way}, device_id_type=MESH))
            return self

        def start(self, there):
            @pl.when(there)
            def _():
                for copy in self.copies:
                    copy.start()

        def arrive(self, there):
            pl.when(there)(lambda: wait_rows(self.amount, self.recv))

    def out_rows(way, near, far):
        return slice(y2 - far, y2 - near) if way == 1 else slice(y1 + near, y1 + far)

    def in_rows(way, near, far):
        return slice(y1 - far, y1 - near) if way == 1 else slice(y2 + near, y2 + far)

    def out_planes(way, near, far):
        return pl.ds(jnp.where(way == 1, x2 - far, x1 + near), far - near)

    def in_planes(way, near, far):
        return pl.ds(jnp.where(way == 1, x1 - far, x2 + near), far - near)

    def over_y(group, way, fs, planes, near, far):
        a, b = out_rows(way, near, far), in_rows(way, near, far)
        group.add(got.at[fs, a, planes], got.at[fs, b, planes], "gy", way)

    sides = (-1, 1)
    everything = slice(0, 9)
    labels_y, labels_x, early, late, faces, corner_labels, corners = {}, {}, {}, {}, {}, {}, {}
    for s, way in enumerate(sides):
        labels_y[way] = Group(s, s).add(
            tissue.at[out_rows(way, 0, 3), x1:x2], tissue.at[in_rows(way, 0, 3), x1:x2], "gy", way)
        for a in (x1,) if way == 1 else (x1, x2 - 1):
            labels_y[way].add(tissue.at[out_rows(way, 3, 4), a:a + 1], tissue.at[in_rows(way, 3, 4), a:a + 1], "gy", way)
        a, b = (x2 - HALO, x1 - HALO) if way == 1 else (x1, x2)
        labels_x[way] = Group(2 + s, 2 + s).add(
            tissue.at[y1:y2, a:a + HALO], tissue.at[y1:y2, b:b + HALO], "gx", way)
        late[way] = Group(s, 4 + s)
        over_y(late[way], way, slice(0, 6) if way == 1 else everything, slice(x1 + 1, x2 - 1), 2, 3)
        over_y(late[way], way, slice(2, 3) if way == 1 else slice(0, 2), slice(x1, x2), 3, 4)
        over_y(late[way], way, everything, out_planes(ways[0], 2, 4), 1, 2)
        for fs in (slice(0, 4), slice(6, 9)) if way == 1 else (slice(0, 3), slice(4, 9)):
            over_y(late[way], way, fs, out_planes(ways[0], 3, 4), 0, 1)
        faces[way] = Group(2 + s, 6 + s)
        for fs, near, far in ((everything, 0, 3), (slice(0, 1) if way == 1 else slice(1, 3), 3, 4)):
            a, b = (x2 - far, x1 - far) if way == 1 else (x1 + near, x2 + near)
            faces[way].add(got.at[fs, y1:y2, a:a + far - near], got.at[fs, y1:y2, b:b + far - near], "gx", way)
        for k, x_way in enumerate(ways):
            tall = pl.ds(GOT[SXY] if way == 1 else jnp.where(x_way == 1, GOT[SXZ], GOT[SXX]), 1)
            parts = [(everything, 0, 1, 0, 3), (tall, 0, 1, 3, 4)]
            if k == 0:
                wide = pl.ds(jnp.where(x_way == 1, GOT[SXY], GOT[SYZ]) if way == 1 else GOT[SYY], 1)
                parts += [(everything, 1, 2, 0, 2), (everything, 2, 3, 0, 1), (wide, 3, 4, 0, 1)]
            else:
                parts += [(everything, 1, 4, 0, 2)]
            early[k, way] = Group(s, 8 + 2 * k + s)
            corner_labels[k, way] = Group(4 + 2 * k + s, 12 + 2 * k + s).add(
                tissue.at[in_rows(way, 0, 3), out_planes(x_way, 0, 3)],
                tissue.at[in_rows(way, 0, 3), in_planes(x_way, 0, 3)], "gx", x_way)
            corners[k, way] = Group(4 + 2 * k + s, 16 + 2 * k + s)
            for fs, x_near, x_far, near, far in parts:
                over_y(early[k, way], way, (slice(4, 6) if way == 1 else slice(3, 4)) if x_near == 3 else fs, out_planes(x_way, x_near, x_far), near, far)
                corners[k, way].add(
                    got.at[fs, in_rows(way, near, far), out_planes(x_way, x_near, x_far)],
                    got.at[fs, in_rows(way, near, far), in_planes(x_way, x_near, x_far)], "gx", x_way)

    urgent = has_x[0]
    mild = jnp.logical_not(urgent | odd)
    calm = jnp.logical_not(urgent) & odd
    for way in sides:
        early[0, way].start(has["gy", way] & urgent)
    for way in sides:
        labels_y[way].start(has["gy", way])
    for way in sides:
        early[1, way].start(has["gy", way])
    for way in sides:
        early[0, way].start(has["gy", way] & jnp.logical_not(urgent | calm))
    for way in sides:
        labels_x[way].start(has["gx", way])
    for way in sides:
        faces[way].start(has["gx", way])
    for way in sides:
        late[way].start(has["gy", way] & jnp.logical_not(urgent | calm | mild))

    for k in range(2):
        for way in sides:
            early[k, way].arrive(has["gy", -way] & has_x[k])
            corners[k, way].start(has["gy", -way] & has_x[k])
        if k == 0:
            for way in sides:
                late[way].start(has["gy", way] & urgent)
            for way in sides:
                labels_y[way].arrive(has["gy", -way])
                for j in range(2):
                    corner_labels[j, way].start(has["gy", -way] & has_x[j])
            for way in sides:
                late[way].start(has["gy", way] & mild)
    for way in sides:
        early[0, way].start(has["gy", way] & calm)
        late[way].start(has["gy", way] & calm)

    def look_up(first, after):
        @pl.loop(first, after)
        def _(row):
            label = tissue[row, x0:x3]
            tables = [jnp.zeros(label.shape, jnp.float32) for _ in range(4)]
            for kind in range(LABELS):
                here = label == kind
                values = (buoy_t[kind], lame_t[kind], shear_t[kind], 1.0 - relax_t[kind])
                tables = [jnp.where(here, value, old) for value, old in zip(values, tables)]
            for ref, table in zip((buoy, lame, shear, keep), tables):
                ref[row] = table

    def v(k, c, y, move=0, span=whole):
        return vel[3 * (k - 1) + c, y1 + y, span[0] + move:span[1] + move]

    def s(k, f, y, move=0, span=whole):
        part = slice(span[0] + move, span[1] + move)
        return sig[6 * (k - 1) + f - SXX, y1 + y, part] if k else got[GOT[f], y1 + y, part]

    def table(ref, y, span=whole):
        return ref[y1 + y, span[0] - x0:span[1] - x0]

    position = lax.broadcasted_iota(jnp.int32, (x3 - x0, lanes), 0)
    begins = (position == HALO) | (position == HALO + local_x)
    ends = (position == HALO - 1) | (position == HALO + local_x - 1)

    def speed_x(k, y):
        b = table(buoy, y)
        if k == 1:
            more = jnp.where(ends, s(0, SXX, y, 1), 0.0)
            if y in (0, local_y):
                more = more - s(0, SXY, y - 1)
            new = got[GOT[VX], y1 + y, x0:x3] + b * more
        else:
            new = v(k - 1, VX, y) + b * (
                s(k - 1, SXX, y, 1) - s(k - 1, SXX, y) + (s(k - 1, SXY, y) - s(k - 1, SXY, y - 1))
                + behind_z(s(k - 1, SXZ, y)))
        return [(vel, (3 * (k - 1) + VX, y1 + y, slice(x0, x3)), new)]

    def speed_y(k, y):
        b = table(buoy, y)
        if k == 1:
            more = -jnp.where(begins, s(0, SXY, y, -1), 0.0)
            if y in (-1, local_y - 1):
                more = more + s(0, SYY, y + 1)
            new = got[GOT[VY], y1 + y, x0:x3] + b * more
        else:
            new = v(k - 1, VY, y) + b * (
                s(k - 1, SXY, y) - s(k - 1, SXY, y, -1) + (s(k - 1, SYY, y + 1) - s(k - 1, SYY, y))
                + behind_z(s(k - 1, SYZ, y)))
        return [(vel, (3 * (k - 1) + VY, y1 + y, slice(x0, x3)), new)]

    def speed_z(k, y):
        b = table(buoy, y)
        if k == 1:
            more = -jnp.where(begins, s(0, SXZ, y, -1), 0.0)
            if y in (0, local_y):
                more = more - s(0, SYZ, y - 1)
            new = got[GOT[VZ], y1 + y, x0:x3] + b * more
        else:
            new = v(k - 1, VZ, y) + b * (
                s(k - 1, SXZ, y) - s(k - 1, SXZ, y, -1) + (s(k - 1, SYZ, y) - s(k - 1, SYZ, y - 1))
                + ahead_z(s(k - 1, SZZ, y)))
        return [(vel, (3 * (k - 1) + VZ, y1 + y, slice(x0, x3)), new)]

    def stresses(k, y):
        span = mine if k == STEPS else whole
        get = lambda c, row=y, move=0: v(k, c, row, move, span)
        old = lambda f: s(k - 1, f, y, 0, span)
        vx, vy, vz = get(VX), get(VY), get(VZ)
        lam, mu, kept = table(lame, y, span), table(shear, y, span), table(keep, y, span)
        exx, eyy, ezz = vx - get(VX, y, -1), vy - get(VY, y - 1), behind_z(vz)
        spread = lam * (exx + eyy + ezz)
        twice = 2.0 * mu
        new = {
            SXX: kept * old(SXX) + spread + twice * exx,
            SYY: kept * old(SYY) + spread + twice * eyy,
            SZZ: kept * old(SZZ) + spread + twice * ezz,
            SXY: kept * old(SXY) + mu * (get(VX, y + 1) - vx + (get(VY, y, 1) - vy)),
            SXZ: kept * old(SXZ) + mu * (ahead_z(vx) + (get(VZ, y, 1) - vz)),
            SYZ: kept * old(SYZ) + mu * (ahead_z(vy) + (get(VZ, y + 1) - vz)),
        }
        if k == STEPS:
            new.update({VX: vx, VY: vy, VZ: vz})
            return [(out, (pl.ds(f * block + y, local_x, stride=local_y), slice(None)), value)
                    for f, value in new.items()]
        return [(sig, (6 * (k - 1) + f - SXX, y1 + y, slice(x0, x3)), value) for f, value in new.items()]

    def reach(k, low, high, inner):
        known = range(k + low, local_y - k + high)
        if inner:
            return known
        needed = range(k - STEPS + low, local_y + STEPS - k + high)
        return [y for y in needed if y not in known]

    def steps(inner):
        for k in range(1, STEPS + 1):
            each(functools.partial(speed_x, k), reach(k, 0, 1, inner))
            each(functools.partial(speed_z, k), reach(k, 0, 1, inner))
            each(functools.partial(speed_y, k), reach(k, -1, 0, inner))
            each(functools.partial(stresses, k), reach(k, 0, 0, inner))

    for way in sides:
        labels_x[way].arrive(has["gx", -way])
    look_up(y1, y2)
    for way in sides:
        faces[way].arrive(has["gx", -way])
    steps(True)
    for k in range(2):
        for way in sides:
            corner_labels[k, way].arrive(has["gy", -way] & has_x[k])
    look_up(y0, y1)
    look_up(y2, y3)
    for way in sides:
        late[way].arrive(has["gy", -way])
        for k in range(2):
            early[k, way].arrive(has["gy", -way] & jnp.logical_not(has_x[k]))
    for k in range(2):
        for way in sides:
            corners[k, way].arrive(has["gy", -way] & has_x[k])
    steps(False)

    def sent(there, *groups):
        pl.when(there)(lambda: wait_rows(sum(group.amount for group in groups), groups[0].send))

    for way in sides:
        sent(has["gy", way], labels_y[way], early[0, way], early[1, way], late[way])
        sent(has["gx", way], labels_x[way], faces[way])
        for k in range(2):
            sent(has["gy", -way] & has_x[k], corner_labels[k, way], corners[k, way])


def on_device(nx, ny, fields, labels, buoyancy, lame_first, shear_modulus, relax_rate):
    local_x, local_y, lanes = labels.shape
    block = local_x * local_y
    wide = 2 * BASE + local_x + 2 * HALO
    tall = local_y + 2 * HALO
    anywhere = pl.BlockSpec(memory_space=pl.ANY)
    table = pltpu.SMEM((LABELS,), jnp.float32)
    moduli = pltpu.VMEM((tall, local_x + 2 * HALO, lanes), jnp.float32)
    advanced = pl.pallas_call(
        functools.partial(kernel, nx, ny, labels.shape),
        out_shape=pltpu.VMEM((9 * block, lanes), jnp.float32),
        in_specs=[anywhere] * 6,
        out_specs=pl.BlockSpec(memory_space=pltpu.VMEM),
        scratch_shapes=[
            pltpu.VMEM((9 * block, lanes), jnp.float32),
            pltpu.VMEM((block, lanes), jnp.int32),
            pltpu.VMEM((9, tall, wide, lanes), jnp.float32),
            pltpu.VMEM((3 * STEPS, tall, wide, lanes), jnp.float32),
            pltpu.VMEM((6 * STEPS - 6, tall, wide, lanes), jnp.float32),
            pltpu.VMEM((tall, wide, lanes), jnp.int32),
            moduli, moduli, moduli, moduli,
            pltpu.VMEM((6 * block, lanes), jnp.float32),
            table, table, table, table,
            pltpu.SemaphoreType.DMA((8,)),
            pltpu.SemaphoreType.DMA((20,)),
            pltpu.SemaphoreType.DMA((6,)),
        ],
        compiler_params=pltpu.CompilerParams(collective_id=0, has_side_effects=True),
        name="waves",
    )(fields.reshape(9 * block, lanes), labels.reshape(block, lanes), buoyancy, lame_first, shear_modulus, relax_rate)
    return advanced.reshape(fields.shape)


def solution(mesh):
    placed = (P(None, "gx", "gy", None), P("gx", "gy", None), P(), P(), P(), P())
    return jax.shard_map(
        functools.partial(on_device, mesh.shape["gx"], mesh.shape["gy"]),
        mesh=mesh, in_specs=placed, out_specs=P(None, "gx", "gy", None), check_vma=False,
    )
```

```python
import functools

import jax
import jax.numpy as jnp
from jax import lax
from jax.experimental import pallas as pl
from jax.experimental.pallas import tpu as pltpu
from jax.sharding import PartitionSpec as P

STEPS = 4
LABELS = 8
HALO = STEPS
BASE = 8
MESH = pl.DeviceIdType.MESH
VX, VY, VZ, SXX, SYY, SZZ, SXY, SXZ, SYZ = range(9)
GOT = (0, 2, 1, 6, 3, 7, 4, 8, 5)


def kernel(nx, ny, shape, fields, labels, buoy_h, lame_h, shear_h, relax_h, out, flat, flat_labels, got, vel, sig,
           tissue, buoy, lame, shear, keep, count, buoy_t, lame_t, shear_t, relax_t, send_sem, recv_sem, local_sem):
    local_x, local_y, lanes = shape
    block = local_x * local_y
    gx, gy = lax.axis_index("gx"), lax.axis_index("gy")
    has = {("gx", -1): gx > 0, ("gx", 1): gx < nx - 1, ("gy", -1): gy > 0, ("gy", 1): gy < ny - 1}
    place = {"gx": gx, "gy": gy}
    x0, x1, x2, x3 = BASE, BASE + HALO, BASE + HALO + local_x, BASE + local_x + 2 * HALO
    y0, y1, y2, y3 = 0, HALO, HALO + local_y, local_y + 2 * HALO
    whole, mine = (x0, x3), (x1, x2)

    barrier = pltpu.get_barrier_semaphore()
    for (axis, way), there in has.items():
        @pl.when(there)
        def _(axis=axis, way=way):
            pl.semaphore_signal(barrier, inc=1, device_id={axis: place[axis] + way}, device_id_type=MESH)

    copies = [pltpu.make_async_copy(source, target, local_sem.at[index]) for index, (source, target) in enumerate((
        (labels, flat_labels), (buoy_h, buoy_t), (fields, flat), (lame_h, lame_t), (shear_h, shear_t),
        (relax_h, relax_t)))]
    for copy in copies:
        copy.start()

    def wait_rows(amount, sem):
        pltpu.make_async_copy(count.at[:amount], count.at[:amount], sem).wait()

    def blank(a, b, c, d):
        got[:, c:d, a:b] = jnp.zeros((9, d - c, b - a, lanes), jnp.float32)
        tissue[c:d, a:b] = jnp.full((d - c, b - a, lanes), LABELS, jnp.int32)

    pl.when(jnp.logical_not(has["gx", -1]))(lambda: blank(x0, x1, y0, y3))
    pl.when(jnp.logical_not(has["gx", 1]))(lambda: blank(x2, x3, y0, y3))
    pl.when(jnp.logical_not(has["gy", -1]))(lambda: blank(x0, x3, y0, y1))
    pl.when(jnp.logical_not(has["gy", 1]))(lambda: blank(x0, x3, y2, y3))

    lane = lax.broadcasted_iota(jnp.int32, (x3 - x0, lanes), 1)
    first_z, last_z = lane == 0, lane == lanes - 1

    def ahead_z(a):
        following = pltpu.roll(a, lanes - 1, 1)
        return jnp.where(last_z[:a.shape[0]], 0.0, following) - a

    def behind_z(a):
        return a - jnp.where(first_z[:a.shape[0]], 0.0, pltpu.roll(a, 1, 1))

    cell = lax.broadcasted_iota(jnp.int32, (local_x, lanes), 0)
    first_x, last_x = cell == 0, cell == local_x - 1
    copies[0].wait()
    copies[1].wait()
    own_labels = []
    for y in range(local_y):
        label = flat_labels[pl.ds(y, local_x, stride=local_y), :]
        tissue[y1 + y, x1:x2] = label
        table = jnp.zeros(label.shape, jnp.float32)
        for kind in range(LABELS):
            table = jnp.where(label == kind, buoy_t[kind], table)
        buoy[y1 + y, x1 - x0:x2 - x0] = table
    copies[2].wait()

    def alone(y):
        get = lambda f, row=y: flat[pl.ds(f * block + row, local_x, stride=local_y), :]
        b = buoy[y1 + y, x1 - x0:x2 - x0]
        sxx, syy, szz, sxy, sxz, syz = (get(f) for f in range(SXX, SYZ + 1))
        xx = jnp.where(last_x, 0.0, pltpu.roll(sxx, local_x - 1, 0)) - sxx
        xy = sxy - jnp.where(first_x, 0.0, pltpu.roll(sxy, 1, 0))
        xz = sxz - jnp.where(first_x, 0.0, pltpu.roll(sxz, 1, 0))
        yx, yz = (sxy - get(SXY, y - 1), syz - get(SYZ, y - 1)) if y > 0 else (sxy, syz)
        yy = get(SYY, y + 1) - syy if y < local_y - 1 else -syy
        new = {
            VX: get(VX) + b * (xx + yx + behind_z(sxz)),
            VY: get(VY) + b * (xy + yy + behind_z(syz)),
            VZ: get(VZ) + b * (xz + yz + ahead_z(szz)),
            SXX: sxx, SYY: syy, SZZ: szz, SXY: sxy, SXZ: sxz, SYZ: syz,
        }
        return [(got, (GOT[f], y1 + y, slice(x1, x2)), value) for f, value in new.items()]

    def each(body, places, pack=2):
        places = list(places)
        for index in range(0, len(places), pack):
            for ref, where, value in [item for y in places[index:index + pack] for item in body(y)]:
                ref[where] = value

    each(alone, range(local_y))
    for copy in copies[3:]:
        copy.wait()
    pl.semaphore_wait(barrier, sum(there.astype(jnp.int32) for there in has.values()))

    odd = lax.rem(gx, 2) == 1
    ways = (jnp.where(odd, 1, -1), jnp.where(odd, -1, 1))
    has_x = (jnp.where(odd, gx < nx - 1, gx > 0), jnp.where(odd, gx > 0, gx < nx - 1))

    class Group:
        def __init__(self, send, recv):
            self.send, self.recv, self.copies, self.amount = send_sem.at[send], recv_sem.at[recv], [], 0

        def add(self, source, target, axis, way):
            size = 1
            for extent in source.shape[:-1]:
                size *= extent
            self.amount += size
            self.copies.append(pltpu.make_async_remote_copy(
                src_ref=source, dst_ref=target, send_sem=self.send, recv_sem=self.recv,
                device_id={axis: place[axis] + way}, device_id_type=MESH))
            return self

        def start(self, there):
            @pl.when(there)
            def _():
                for copy in self.copies:
                    copy.start()

        def arrive(self, there):
            pl.when(there)(lambda: wait_rows(self.amount, self.recv))

    def out_rows(way, near, far):
        return slice(y2 - far, y2 - near) if way == 1 else slice(y1 + near, y1 + far)

    def in_rows(way, near, far):
        return slice(y1 - far, y1 - near) if way == 1 else slice(y2 + near, y2 + far)

    def out_planes(way, near, far):
        return pl.ds(jnp.where(way == 1, x2 - far, x1 + near), far - near)

    def in_planes(way, near, far):
        return pl.ds(jnp.where(way == 1, x1 - far, x2 + near), far - near)

    def over_y(group, way, fs, planes, near, far):
        a, b = out_rows(way, near, far), in_rows(way, near, far)
        group.add(got.at[fs, a, planes], got.at[fs, b, planes], "gy", way)

    sides = (-1, 1)
    everything = slice(0, 9)
    labels_y, labels_x, early, late, faces, corner_labels, corners = {}, {}, {}, {}, {}, {}, {}
    for s, way in enumerate(sides):
        labels_y[way] = Group(s, s).add(
            tissue.at[out_rows(way, 0, 3), x1:x2], tissue.at[in_rows(way, 0, 3), x1:x2], "gy", way)
        for a in (x1,) if way == 1 else (x1, x2 - 1):
            labels_y[way].add(tissue.at[out_rows(way, 3, 4), a:a + 1], tissue.at[in_rows(way, 3, 4), a:a + 1], "gy", way)
        a, b = (x2 - HALO, x1 - HALO) if way == 1 else (x1, x2)
        labels_x[way] = Group(2 + s, 2 + s).add(
            tissue.at[y1:y2, a:a + HALO], tissue.at[y1:y2, b:b + HALO], "gx", way)
        late[way] = Group(s, 4 + s)
        over_y(late[way], way, slice(0, 6) if way == 1 else everything, slice(x1 + 1, x2 - 1), 2, 3)
        over_y(late[way], way, slice(2, 3) if way == 1 else slice(0, 2), slice(x1, x2), 3, 4)
        for x_way in ways:
            over_y(late[way], way, everything, out_planes(x_way, 2, 4), 1, 2)
            for fs in (slice(0, 4), slice(6, 9)) if way == 1 else (slice(0, 3), slice(4, 9)):
                over_y(late[way], way, fs, out_planes(x_way, 3, 4), 0, 1)
        faces[way] = Group(2 + s, 6 + s)
        for fs, near, far in ((everything, 0, 3), (slice(0, 1) if way == 1 else slice(1, 3), 3, 4)):
            a, b = (x2 - far, x1 - far) if way == 1 else (x1 + near, x2 + near)
            faces[way].add(got.at[fs, y1:y2, a:a + far - near], got.at[fs, y1:y2, b:b + far - near], "gx", way)
        for k, x_way in enumerate(ways):
            tall = pl.ds(GOT[SXY] if way == 1 else jnp.where(x_way == 1, GOT[SXZ], GOT[SXX]), 1)
            parts = [(everything, 0, 1, 0, 3), (tall, 0, 1, 3, 4)]
            wide = pl.ds(jnp.where(x_way == 1, GOT[SXY], GOT[SYZ]) if way == 1 else GOT[SYY], 1)
            parts += [(everything, 1, 2, 0, 2), (everything, 2, 3, 0, 1), (wide, 3, 4, 0, 1)]
            early[k, way] = Group(s, 8 + 2 * k + s)
            corner_labels[k, way] = Group(4 + 2 * k + s, 12 + 2 * k + s).add(
                tissue.at[in_rows(way, 0, 3), out_planes(x_way, 0, 3)],
                tissue.at[in_rows(way, 0, 3), in_planes(x_way, 0, 3)], "gx", x_way)
            corners[k, way] = Group(4 + 2 * k + s, 16 + 2 * k + s)
            for fs, x_near, x_far, near, far in parts:
                over_y(early[k, way], way, (slice(4, 6) if way == 1 else slice(3, 4)) if x_near == 3 else fs, out_planes(x_way, x_near, x_far), near, far)
                corners[k, way].add(
                    got.at[fs, in_rows(way, near, far), out_planes(x_way, x_near, x_far)],
                    got.at[fs, in_rows(way, near, far), in_planes(x_way, x_near, x_far)], "gx", x_way)

    urgent = has_x[0]
    calm = jnp.logical_not(urgent) & odd
    for way in sides:
        early[0, way].start(has["gy", way] & urgent)
    for way in sides:
        labels_y[way].start(has["gy", way])
    for way in sides:
        early[1, way].start(has["gy", way])
    for way in sides:
        early[0, way].start(has["gy", way] & jnp.logical_not(urgent | calm))
    for way in sides:
        labels_x[way].start(has["gx", way])
    for way in sides:
        faces[way].start(has["gx", way])
    for way in sides:
        late[way].start(has["gy", way] & jnp.logical_not(urgent | calm))

    for k in range(2):
        for way in sides:
            early[k, way].arrive(has["gy", -way] & has_x[k])
            corners[k, way].start(has["gy", -way] & has_x[k])
        if k == 0:
            for way in sides:
                late[way].start(has["gy", way] & urgent)
            for way in sides:
                labels_y[way].arrive(has["gy", -way])
                for j in range(2):
                    corner_labels[j, way].start(has["gy", -way] & has_x[j])
    for way in sides:
        early[0, way].start(has["gy", way] & calm)
        late[way].start(has["gy", way] & calm)

    def look_up(first, after):
        @pl.loop(first, after)
        def _(row):
            label = tissue[row, x0:x3]
            tables = [jnp.zeros(label.shape, jnp.float32) for _ in range(4)]
            for kind in range(LABELS):
                here = label == kind
                values = (buoy_t[kind], lame_t[kind], shear_t[kind], 1.0 - relax_t[kind])
                tables = [jnp.where(here, value, old) for value, old in zip(values, tables)]
            for ref, table in zip((buoy, lame, shear, keep), tables):
                ref[row] = table

    def v(k, c, y, move=0, span=whole):
        return vel[3 * (k - 1) + c, y1 + y, span[0] + move:span[1] + move]

    def s(k, f, y, move=0, span=whole):
        part = slice(span[0] + move, span[1] + move)
        return sig[6 * (k - 1) + f - SXX, y1 + y, part] if k else got[GOT[f], y1 + y, part]

    def table(ref, y, span=whole):
        return ref[y1 + y, span[0] - x0:span[1] - x0]

    position = lax.broadcasted_iota(jnp.int32, (x3 - x0, lanes), 0)
    begins = (position == HALO) | (position == HALO + local_x)
    ends = (position == HALO - 1) | (position == HALO + local_x - 1)

    def speed_x(k, y):
        b = table(buoy, y)
        if k == 1:
            more = jnp.where(ends, s(0, SXX, y, 1), 0.0)
            if y in (0, local_y):
                more = more - s(0, SXY, y - 1)
            new = got[GOT[VX], y1 + y, x0:x3] + b * more
        else:
            new = v(k - 1, VX, y) + b * (
                s(k - 1, SXX, y, 1) - s(k - 1, SXX, y) + (s(k - 1, SXY, y) - s(k - 1, SXY, y - 1))
                + behind_z(s(k - 1, SXZ, y)))
        return [(vel, (3 * (k - 1) + VX, y1 + y, slice(x0, x3)), new)]

    def speed_y(k, y):
        b = table(buoy, y)
        if k == 1:
            more = -jnp.where(begins, s(0, SXY, y, -1), 0.0)
            if y in (-1, local_y - 1):
                more = more + s(0, SYY, y + 1)
            new = got[GOT[VY], y1 + y, x0:x3] + b * more
        else:
            new = v(k - 1, VY, y) + b * (
                s(k - 1, SXY, y) - s(k - 1, SXY, y, -1) + (s(k - 1, SYY, y + 1) - s(k - 1, SYY, y))
                + behind_z(s(k - 1, SYZ, y)))
        return [(vel, (3 * (k - 1) + VY, y1 + y, slice(x0, x3)), new)]

    def speed_z(k, y):
        b = table(buoy, y)
        if k == 1:
            more = -jnp.where(begins, s(0, SXZ, y, -1), 0.0)
            if y in (0, local_y):
                more = more - s(0, SYZ, y - 1)
            new = got[GOT[VZ], y1 + y, x0:x3] + b * more
        else:
            new = v(k - 1, VZ, y) + b * (
                s(k - 1, SXZ, y) - s(k - 1, SXZ, y, -1) + (s(k - 1, SYZ, y) - s(k - 1, SYZ, y - 1))
                + ahead_z(s(k - 1, SZZ, y)))
        return [(vel, (3 * (k - 1) + VZ, y1 + y, slice(x0, x3)), new)]

    def stresses(k, y):
        span = mine if k == STEPS else whole
        get = lambda c, row=y, move=0: v(k, c, row, move, span)
        old = lambda f: s(k - 1, f, y, 0, span)
        vx, vy, vz = get(VX), get(VY), get(VZ)
        lam, mu, kept = table(lame, y, span), table(shear, y, span), table(keep, y, span)
        exx, eyy, ezz = vx - get(VX, y, -1), vy - get(VY, y - 1), behind_z(vz)
        spread = lam * (exx + eyy + ezz)
        twice = 2.0 * mu
        new = {
            SXX: kept * old(SXX) + spread + twice * exx,
            SYY: kept * old(SYY) + spread + twice * eyy,
            SZZ: kept * old(SZZ) + spread + twice * ezz,
            SXY: kept * old(SXY) + mu * (get(VX, y + 1) - vx + (get(VY, y, 1) - vy)),
            SXZ: kept * old(SXZ) + mu * (ahead_z(vx) + (get(VZ, y, 1) - vz)),
            SYZ: kept * old(SYZ) + mu * (ahead_z(vy) + (get(VZ, y + 1) - vz)),
        }
        if k == STEPS:
            new.update({VX: vx, VY: vy, VZ: vz})
            return [(out, (pl.ds(f * block + y, local_x, stride=local_y), slice(None)), value)
                    for f, value in new.items()]
        return [(sig, (6 * (k - 1) + f - SXX, y1 + y, slice(x0, x3)), value) for f, value in new.items()]

    def reach(k, low, high, inner):
        known = range(k + low, local_y - k + high)
        if inner:
            return known
        needed = range(k - STEPS + low, local_y + STEPS - k + high)
        return [y for y in needed if y not in known]

    def steps(inner):
        for k in range(1, STEPS + 1):
            each(functools.partial(speed_x, k), reach(k, 0, 1, inner))
            each(functools.partial(speed_z, k), reach(k, 0, 1, inner))
            each(functools.partial(speed_y, k), reach(k, -1, 0, inner))
            each(functools.partial(stresses, k), reach(k, 0, 0, inner))

    for way in sides:
        labels_x[way].arrive(has["gx", -way])
    look_up(y1, y2)
    for way in sides:
        faces[way].arrive(has["gx", -way])
    steps(True)
    for k in range(2):
        for way in sides:
            corner_labels[k, way].arrive(has["gy", -way] & has_x[k])
    look_up(y0, y1)
    look_up(y2, y3)
    for way in sides:
        late[way].arrive(has["gy", -way])
        for k in range(2):
            early[k, way].arrive(has["gy", -way] & jnp.logical_not(has_x[k]))
    for k in range(2):
        for way in sides:
            corners[k, way].arrive(has["gy", -way] & has_x[k])
    steps(False)

    def sent(there, *groups):
        pl.when(there)(lambda: wait_rows(sum(group.amount for group in groups), groups[0].send))

    for way in sides:
        sent(has["gy", way], labels_y[way], early[0, way], early[1, way], late[way])
        sent(has["gx", way], labels_x[way], faces[way])
        for k in range(2):
            sent(has["gy", -way] & has_x[k], corner_labels[k, way], corners[k, way])


def on_device(nx, ny, fields, labels, buoyancy, lame_first, shear_modulus, relax_rate):
    local_x, local_y, lanes = labels.shape
    block = local_x * local_y
    wide = 2 * BASE + local_x + 2 * HALO
    tall = local_y + 2 * HALO
    anywhere = pl.BlockSpec(memory_space=pl.ANY)
    table = pltpu.SMEM((LABELS,), jnp.float32)
    moduli = pltpu.VMEM((tall, local_x + 2 * HALO, lanes), jnp.float32)
    advanced = pl.pallas_call(
        functools.partial(kernel, nx, ny, labels.shape),
        out_shape=pltpu.VMEM((9 * block, lanes), jnp.float32),
        in_specs=[anywhere] * 6,
        out_specs=pl.BlockSpec(memory_space=pltpu.VMEM),
        scratch_shapes=[
            pltpu.VMEM((9 * block, lanes), jnp.float32),
            pltpu.VMEM((block, lanes), jnp.int32),
            pltpu.VMEM((9, tall, wide, lanes), jnp.float32),
            pltpu.VMEM((3 * STEPS, tall, wide, lanes), jnp.float32),
            pltpu.VMEM((6 * STEPS - 6, tall, wide, lanes), jnp.float32),
            pltpu.VMEM((tall, wide, lanes), jnp.int32),
            moduli, moduli, moduli, moduli,
            pltpu.VMEM((6 * block, lanes), jnp.float32),
            table, table, table, table,
            pltpu.SemaphoreType.DMA((8,)),
            pltpu.SemaphoreType.DMA((20,)),
            pltpu.SemaphoreType.DMA((6,)),
        ],
        compiler_params=pltpu.CompilerParams(collective_id=0, has_side_effects=True),
        name="waves",
    )(fields.reshape(9 * block, lanes), labels.reshape(block, lanes), buoyancy, lame_first, shear_modulus, relax_rate)
    return advanced.reshape(fields.shape)


def solution(mesh):
    placed = (P(None, "gx", "gy", None), P("gx", "gy", None), P(), P(), P(), P())
    return jax.shard_map(
        functools.partial(on_device, mesh.shape["gx"], mesh.shape["gy"]),
        mesh=mesh, in_specs=placed, out_specs=P(None, "gx", "gy", None), check_vma=False,
    )
```

```python
import functools

import jax
import jax.numpy as jnp
from jax import lax
from jax.experimental import pallas as pl
from jax.experimental.pallas import tpu as pltpu
from jax.sharding import PartitionSpec as P

STEPS = 4
LABELS = 8
HALO = STEPS
BASE = 8
MESH = pl.DeviceIdType.MESH
VX, VY, VZ, SXX, SYY, SZZ, SXY, SXZ, SYZ = range(9)
GOT = (0, 2, 1, 6, 3, 7, 4, 8, 5)


def kernel(nx, ny, shape, fields, labels, buoy_h, lame_h, shear_h, relax_h, out, flat, flat_labels, got, vel, sig,
           tissue, buoy, lame, shear, keep, count, buoy_t, lame_t, shear_t, relax_t, send_sem, recv_sem, local_sem):
    local_x, local_y, lanes = shape
    block = local_x * local_y
    gx, gy = lax.axis_index("gx"), lax.axis_index("gy")
    has = {("gx", -1): gx > 0, ("gx", 1): gx < nx - 1, ("gy", -1): gy > 0, ("gy", 1): gy < ny - 1}
    place = {"gx": gx, "gy": gy}
    x0, x1, x2, x3 = BASE, BASE + HALO, BASE + HALO + local_x, BASE + local_x + 2 * HALO
    y0, y1, y2, y3 = 0, HALO, HALO + local_y, local_y + 2 * HALO
    whole, mine = (x0, x3), (x1, x2)

    barrier = pltpu.get_barrier_semaphore()
    for (axis, way), there in has.items():
        @pl.when(there)
        def _(axis=axis, way=way):
            pl.semaphore_signal(barrier, inc=1, device_id={axis: place[axis] + way}, device_id_type=MESH)

    copies = [pltpu.make_async_copy(source, target, local_sem.at[index]) for index, (source, target) in enumerate((
        (labels, flat_labels), (buoy_h, buoy_t), (fields, flat), (lame_h, lame_t), (shear_h, shear_t),
        (relax_h, relax_t)))]
    for copy in copies:
        copy.start()

    def wait_rows(amount, sem):
        pltpu.make_async_copy(count.at[:amount], count.at[:amount], sem).wait()

    def blank(a, b, c, d):
        got[:, c:d, a:b] = jnp.zeros((9, d - c, b - a, lanes), jnp.float32)
        tissue[c:d, a:b] = jnp.full((d - c, b - a, lanes), LABELS, jnp.int32)

    pl.when(jnp.logical_not(has["gx", -1]))(lambda: blank(x0, x1, y0, y3))
    pl.when(jnp.logical_not(has["gx", 1]))(lambda: blank(x2, x3, y0, y3))
    pl.when(jnp.logical_not(has["gy", -1]))(lambda: blank(x0, x3, y0, y1))
    pl.when(jnp.logical_not(has["gy", 1]))(lambda: blank(x0, x3, y2, y3))

    lane = lax.broadcasted_iota(jnp.int32, (x3 - x0, lanes), 1)
    first_z, last_z = lane == 0, lane == lanes - 1

    def ahead_z(a):
        following = pltpu.roll(a, lanes - 1, 1)
        return jnp.where(last_z[:a.shape[0]], 0.0, following) - a

    def behind_z(a):
        return a - jnp.where(first_z[:a.shape[0]], 0.0, pltpu.roll(a, 1, 1))

    cell = lax.broadcasted_iota(jnp.int32, (local_x, lanes), 0)
    first_x, last_x = cell == 0, cell == local_x - 1
    copies[0].wait()
    copies[1].wait()
    own_labels = []
    for y in range(local_y):
        label = flat_labels[pl.ds(y, local_x, stride=local_y), :]
        tissue[y1 + y, x1:x2] = label
        table = jnp.zeros(label.shape, jnp.float32)
        for kind in range(LABELS):
            table = jnp.where(label == kind, buoy_t[kind], table)
        buoy[y1 + y, x1 - x0:x2 - x0] = table
    copies[2].wait()

    def alone(y):
        get = lambda f, row=y: flat[pl.ds(f * block + row, local_x, stride=local_y), :]
        b = buoy[y1 + y, x1 - x0:x2 - x0]
        sxx, syy, szz, sxy, sxz, syz = (get(f) for f in range(SXX, SYZ + 1))
        xx = jnp.where(last_x, 0.0, pltpu.roll(sxx, local_x - 1, 0)) - sxx
        xy = sxy - jnp.where(first_x, 0.0, pltpu.roll(sxy, 1, 0))
        xz = sxz - jnp.where(first_x, 0.0, pltpu.roll(sxz, 1, 0))
        yx, yz = (sxy - get(SXY, y - 1), syz - get(SYZ, y - 1)) if y > 0 else (sxy, syz)
        yy = get(SYY, y + 1) - syy if y < local_y - 1 else -syy
        new = {
            VX: get(VX) + b * (xx + yx + behind_z(sxz)),
            VY: get(VY) + b * (xy + yy + behind_z(syz)),
            VZ: get(VZ) + b * (xz + yz + ahead_z(szz)),
            SXX: sxx, SYY: syy, SZZ: szz, SXY: sxy, SXZ: sxz, SYZ: syz,
        }
        return [(got, (GOT[f], y1 + y, slice(x1, x2)), value) for f, value in new.items()]

    def each(body, places, pack=2):
        places = list(places)
        for index in range(0, len(places), pack):
            for ref, where, value in [item for y in places[index:index + pack] for item in body(y)]:
                ref[where] = value

    each(alone, range(local_y))
    for copy in copies[3:]:
        copy.wait()
    pl.semaphore_wait(barrier, sum(there.astype(jnp.int32) for there in has.values()))

    odd = lax.rem(gx, 2) == 1
    ways = (jnp.where(odd, 1, -1), jnp.where(odd, -1, 1))
    has_x = (jnp.where(odd, gx < nx - 1, gx > 0), jnp.where(odd, gx > 0, gx < nx - 1))

    class Group:
        def __init__(self, send, recv):
            self.send, self.recv, self.copies, self.amount = send_sem.at[send], recv_sem.at[recv], [], 0

        def add(self, source, target, axis, way):
            size = 1
            for extent in source.shape[:-1]:
                size *= extent
            self.amount += size
            self.copies.append(pltpu.make_async_remote_copy(
                src_ref=source, dst_ref=target, send_sem=self.send, recv_sem=self.recv,
                device_id={axis: place[axis] + way}, device_id_type=MESH))
            return self

        def start(self, there):
            @pl.when(there)
            def _():
                for copy in self.copies:
                    copy.start()

        def arrive(self, there):
            pl.when(there)(lambda: wait_rows(self.amount, self.recv))

    def out_rows(way, near, far):
        return slice(y2 - far, y2 - near) if way == 1 else slice(y1 + near, y1 + far)

    def in_rows(way, near, far):
        return slice(y1 - far, y1 - near) if way == 1 else slice(y2 + near, y2 + far)

    def out_planes(way, near, far):
        return pl.ds(jnp.where(way == 1, x2 - far, x1 + near), far - near)

    def in_planes(way, near, far):
        return pl.ds(jnp.where(way == 1, x1 - far, x2 + near), far - near)

    def over_y(group, way, fs, planes, near, far):
        a, b = out_rows(way, near, far), in_rows(way, near, far)
        group.add(got.at[fs, a, planes], got.at[fs, b, planes], "gy", way)

    sides = (-1, 1)
    everything = slice(0, 9)
    labels_y, labels_x, early, late, faces, corner_labels, corners = {}, {}, {}, {}, {}, {}, {}
    for s, way in enumerate(sides):
        labels_y[way] = Group(s, s).add(
            tissue.at[out_rows(way, 0, 3), x1:x2], tissue.at[in_rows(way, 0, 3), x1:x2], "gy", way)
        for a in (x1,) if way == 1 else (x1, x2 - 1):
            labels_y[way].add(tissue.at[out_rows(way, 3, 4), a:a + 1], tissue.at[in_rows(way, 3, 4), a:a + 1], "gy", way)
        a, b = (x2 - HALO, x1 - HALO) if way == 1 else (x1, x2)
        labels_x[way] = Group(2 + s, 2 + s).add(
            tissue.at[y1:y2, a:a + HALO], tissue.at[y1:y2, b:b + HALO], "gx", way)
        late[way] = Group(s, 4 + s)
        over_y(late[way], way, slice(0, 6) if way == 1 else everything, slice(x1 + 1, x2 - 1), 2, 3)
        over_y(late[way], way, slice(2, 3) if way == 1 else slice(0, 2), slice(x1, x2), 3, 4)
        for x_way in ways:
            over_y(late[way], way, everything, out_planes(x_way, 2, 4), 1, 2)
            for fs in (slice(0, 4), slice(6, 9)) if way == 1 else (slice(0, 3), slice(4, 9)):
                over_y(late[way], way, fs, out_planes(x_way, 3, 4), 0, 1)
        faces[way] = Group(2 + s, 6 + s)
        for fs, near, far in ((everything, 0, 3), (slice(0, 1) if way == 1 else slice(1, 3), 3, 4)):
            a, b = (x2 - far, x1 - far) if way == 1 else (x1 + near, x2 + near)
            faces[way].add(got.at[fs, y1:y2, a:a + far - near], got.at[fs, y1:y2, b:b + far - near], "gx", way)
        for k, x_way in enumerate(ways):
            tall = pl.ds(GOT[SXY] if way == 1 else jnp.where(x_way == 1, GOT[SXZ], GOT[SXX]), 1)
            parts = [(everything, 0, 1, 0, 3), (tall, 0, 1, 3, 4)]
            wide = pl.ds(jnp.where(x_way == 1, GOT[SXY], GOT[SYZ]) if way == 1 else GOT[SYY], 1)
            parts += [(everything, 1, 2, 0, 2), (everything, 2, 3, 0, 1), (wide, 3, 4, 0, 1)]
            early[k, way] = Group(s, 8 + 2 * k + s)
            corner_labels[k, way] = Group(4 + 2 * k + s, 12 + 2 * k + s).add(
                tissue.at[in_rows(way, 0, 3), out_planes(x_way, 0, 3)],
                tissue.at[in_rows(way, 0, 3), in_planes(x_way, 0, 3)], "gx", x_way)
            corners[k, way] = Group(4 + 2 * k + s, 16 + 2 * k + s)
            for fs, x_near, x_far, near, far in parts:
                over_y(early[k, way], way, (slice(4, 6) if way == 1 else slice(3, 4)) if x_near == 3 else fs, out_planes(x_way, x_near, x_far), near, far)
                corners[k, way].add(
                    got.at[fs, in_rows(way, near, far), out_planes(x_way, x_near, x_far)],
                    got.at[fs, in_rows(way, near, far), in_planes(x_way, x_near, x_far)], "gx", x_way)

    urgent = has_x[0]
    held = urgent & jnp.logical_not(odd)
    calm = jnp.logical_not(urgent) & odd
    for way in sides:
        early[0, way].start(has["gy", way] & urgent)
    for way in sides:
        labels_y[way].start(has["gy", way])
    for way in sides:
        early[1, way].start(has["gy", way])
    for way in sides:
        early[0, way].start(has["gy", way] & jnp.logical_not(urgent | calm))
    for way in sides:
        labels_x[way].start(has["gx", way])
    for way in sides:
        faces[way].start(has["gx", way])
    for way in sides:
        late[way].start(has["gy", way] & jnp.logical_not(held | calm))

    for k in range(2):
        for way in sides:
            early[k, way].arrive(has["gy", -way] & has_x[k])
            corners[k, way].start(has["gy", -way] & has_x[k])
        if k == 0:
            for way in sides:
                late[way].start(has["gy", way] & held)
            for way in sides:
                labels_y[way].arrive(has["gy", -way])
                for j in range(2):
                    corner_labels[j, way].start(has["gy", -way] & has_x[j])
    for way in sides:
        early[0, way].start(has["gy", way] & calm)
        late[way].start(has["gy", way] & calm)

    def look_up(first, after):
        @pl.loop(first, after)
        def _(row):
            label = tissue[row, x0:x3]
            tables = [jnp.zeros(label.shape, jnp.float32) for _ in range(4)]
            for kind in range(LABELS):
                here = label == kind
                values = (buoy_t[kind], lame_t[kind], shear_t[kind], 1.0 - relax_t[kind])
                tables = [jnp.where(here, value, old) for value, old in zip(values, tables)]
            for ref, table in zip((buoy, lame, shear, keep), tables):
                ref[row] = table

    def v(k, c, y, move=0, span=whole):
        return vel[3 * (k - 1) + c, y1 + y, span[0] + move:span[1] + move]

    def s(k, f, y, move=0, span=whole):
        part = slice(span[0] + move, span[1] + move)
        return sig[6 * (k - 1) + f - SXX, y1 + y, part] if k else got[GOT[f], y1 + y, part]

    def table(ref, y, span=whole):
        return ref[y1 + y, span[0] - x0:span[1] - x0]

    position = lax.broadcasted_iota(jnp.int32, (x3 - x0, lanes), 0)
    begins = (position == HALO) | (position == HALO + local_x)
    ends = (position == HALO - 1) | (position == HALO + local_x - 1)

    def speed_x(k, y):
        b = table(buoy, y)
        if k == 1:
            more = jnp.where(ends, s(0, SXX, y, 1), 0.0)
            if y in (0, local_y):
                more = more - s(0, SXY, y - 1)
            new = got[GOT[VX], y1 + y, x0:x3] + b * more
        else:
            new = v(k - 1, VX, y) + b * (
                s(k - 1, SXX, y, 1) - s(k - 1, SXX, y) + (s(k - 1, SXY, y) - s(k - 1, SXY, y - 1))
                + behind_z(s(k - 1, SXZ, y)))
        return [(vel, (3 * (k - 1) + VX, y1 + y, slice(x0, x3)), new)]

    def speed_y(k, y):
        b = table(buoy, y)
        if k == 1:
            more = -jnp.where(begins, s(0, SXY, y, -1), 0.0)
            if y in (-1, local_y - 1):
                more = more + s(0, SYY, y + 1)
            new = got[GOT[VY], y1 + y, x0:x3] + b * more
        else:
            new = v(k - 1, VY, y) + b * (
                s(k - 1, SXY, y) - s(k - 1, SXY, y, -1) + (s(k - 1, SYY, y + 1) - s(k - 1, SYY, y))
                + behind_z(s(k - 1, SYZ, y)))
        return [(vel, (3 * (k - 1) + VY, y1 + y, slice(x0, x3)), new)]

    def speed_z(k, y):
        b = table(buoy, y)
        if k == 1:
            more = -jnp.where(begins, s(0, SXZ, y, -1), 0.0)
            if y in (0, local_y):
                more = more - s(0, SYZ, y - 1)
            new = got[GOT[VZ], y1 + y, x0:x3] + b * more
        else:
            new = v(k - 1, VZ, y) + b * (
                s(k - 1, SXZ, y) - s(k - 1, SXZ, y, -1) + (s(k - 1, SYZ, y) - s(k - 1, SYZ, y - 1))
                + ahead_z(s(k - 1, SZZ, y)))
        return [(vel, (3 * (k - 1) + VZ, y1 + y, slice(x0, x3)), new)]

    def stresses(k, y):
        span = mine if k == STEPS else whole
        get = lambda c, row=y, move=0: v(k, c, row, move, span)
        old = lambda f: s(k - 1, f, y, 0, span)
        vx, vy, vz = get(VX), get(VY), get(VZ)
        lam, mu, kept = table(lame, y, span), table(shear, y, span), table(keep, y, span)
        exx, eyy, ezz = vx - get(VX, y, -1), vy - get(VY, y - 1), behind_z(vz)
        spread = lam * (exx + eyy + ezz)
        twice = 2.0 * mu
        new = {
            SXX: kept * old(SXX) + spread + twice * exx,
            SYY: kept * old(SYY) + spread + twice * eyy,
            SZZ: kept * old(SZZ) + spread + twice * ezz,
            SXY: kept * old(SXY) + mu * (get(VX, y + 1) - vx + (get(VY, y, 1) - vy)),
            SXZ: kept * old(SXZ) + mu * (ahead_z(vx) + (get(VZ, y, 1) - vz)),
            SYZ: kept * old(SYZ) + mu * (ahead_z(vy) + (get(VZ, y + 1) - vz)),
        }
        if k == STEPS:
            new.update({VX: vx, VY: vy, VZ: vz})
            return [(out, (pl.ds(f * block + y, local_x, stride=local_y), slice(None)), value)
                    for f, value in new.items()]
        return [(sig, (6 * (k - 1) + f - SXX, y1 + y, slice(x0, x3)), value) for f, value in new.items()]

    def reach(k, low, high, inner):
        known = range(k + low, local_y - k + high)
        if inner:
            return known
        needed = range(k - STEPS + low, local_y + STEPS - k + high)
        return [y for y in needed if y not in known]

    def steps(inner):
        for k in range(1, STEPS + 1):
            each(functools.partial(speed_x, k), reach(k, 0, 1, inner))
            each(functools.partial(speed_z, k), reach(k, 0, 1, inner))
            each(functools.partial(speed_y, k), reach(k, -1, 0, inner))
            each(functools.partial(stresses, k), reach(k, 0, 0, inner))

    for way in sides:
        labels_x[way].arrive(has["gx", -way])
    look_up(y1, y2)
    for way in sides:
        faces[way].arrive(has["gx", -way])
    steps(True)
    for k in range(2):
        for way in sides:
            corner_labels[k, way].arrive(has["gy", -way] & has_x[k])
    look_up(y0, y1)
    look_up(y2, y3)
    for way in sides:
        late[way].arrive(has["gy", -way])
        for k in range(2):
            early[k, way].arrive(has["gy", -way] & jnp.logical_not(has_x[k]))
    for k in range(2):
        for way in sides:
            corners[k, way].arrive(has["gy", -way] & has_x[k])
    steps(False)

    def sent(there, *groups):
        pl.when(there)(lambda: wait_rows(sum(group.amount for group in groups), groups[0].send))

    for way in sides:
        sent(has["gy", way], labels_y[way], early[0, way], early[1, way], late[way])
        sent(has["gx", way], labels_x[way], faces[way])
        for k in range(2):
            sent(has["gy", -way] & has_x[k], corner_labels[k, way], corners[k, way])


def on_device(nx, ny, fields, labels, buoyancy, lame_first, shear_modulus, relax_rate):
    local_x, local_y, lanes = labels.shape
    block = local_x * local_y
    wide = 2 * BASE + local_x + 2 * HALO
    tall = local_y + 2 * HALO
    anywhere = pl.BlockSpec(memory_space=pl.ANY)
    table = pltpu.SMEM((LABELS,), jnp.float32)
    moduli = pltpu.VMEM((tall, local_x + 2 * HALO, lanes), jnp.float32)
    advanced = pl.pallas_call(
        functools.partial(kernel, nx, ny, labels.shape),
        out_shape=pltpu.VMEM((9 * block, lanes), jnp.float32),
        in_specs=[anywhere] * 6,
        out_specs=pl.BlockSpec(memory_space=pltpu.VMEM),
        scratch_shapes=[
            pltpu.VMEM((9 * block, lanes), jnp.float32),
            pltpu.VMEM((block, lanes), jnp.int32),
            pltpu.VMEM((9, tall, wide, lanes), jnp.float32),
            pltpu.VMEM((3 * STEPS, tall, wide, lanes), jnp.float32),
            pltpu.VMEM((6 * STEPS - 6, tall, wide, lanes), jnp.float32),
            pltpu.VMEM((tall, wide, lanes), jnp.int32),
            moduli, moduli, moduli, moduli,
            pltpu.VMEM((6 * block, lanes), jnp.float32),
            table, table, table, table,
            pltpu.SemaphoreType.DMA((8,)),
            pltpu.SemaphoreType.DMA((20,)),
            pltpu.SemaphoreType.DMA((6,)),
        ],
        compiler_params=pltpu.CompilerParams(collective_id=0, has_side_effects=True),
        name="waves",
    )(fields.reshape(9 * block, lanes), labels.reshape(block, lanes), buoyancy, lame_first, shear_modulus, relax_rate)
    return advanced.reshape(fields.shape)


def solution(mesh):
    placed = (P(None, "gx", "gy", None), P("gx", "gy", None), P(), P(), P(), P())
    return jax.shard_map(
        functools.partial(on_device, mesh.shape["gx"], mesh.shape["gy"]),
        mesh=mesh, in_specs=placed, out_specs=P(None, "gx", "gy", None), check_vma=False,
    )
```
